256 devices in a mesh: col: 64 (over y, z, core), row: 4 (over x).
Axes of the slice: x: 4, y: 4, z: 8, core: 2. Of those that a mesh axis runs over, the one named last changes fastest.
Arguments:
- latent: float32 [32768, 128], P('col'), may hold values from -6 to 6
- v_basis: float32 [64, 4, 128, 48, 256], P(None, 'row', 'col'), may hold values from -0.375 to 0.375
- u_basis: float32 [64, 4, 256, 6144], P('col', 'row'), may hold values from -0.078125 to 0.078125
- ranks: int32 [64, 4, 128], P(None, 'row', 'col'), may hold values from 8 to 48, as said below
- slot_row: int32 [4, 64], P('row'), may hold values from 0 to 63, each once within a row
- wells: int32 [64, 4, 64], P('col', 'row'), may hold values from 0 to 255
- observed: float32 [64, 4, 64, 128], P('col', 'row'), may hold values from 0.3 to 2.5
Outputs:
- field: float32 [64, 4, 256, 128], P('col', 'row')
- gradient: float32 [32768, 128], P(('col', 'row'))
The draws below stay inside these ranges and needn't reach their ends.
Inputs may be any that keep to these rules, and one draw needn't show every extreme that they name: Each row of slot_row is a permutation of 0 .. 63. For every tile row, class and pair of tile columns 2i, 2i + 1, the two ranks sum to at most 72; in every class some pair reaches 72. `wells`: cells may repeat within a slot.
All inputs are finite; a program needn't handle non-finite values.
Results may differ from the reference program's by a relative error of at most 0.0003.
Values sent between devices are 32-bit elements; how exact they have to be, the bound alone decides.
A program may use at most 128 MiB of HBM per device.

```python
import jax
import jax.numpy as jnp
from jax import lax

B = 256
K = 48
S = 128
WPT = 64
RPAIR = 72
TC = 128
RQ = 64
N_COL = 64
N_ROW = 4


def draw_ranks(key, part):
    lowest = K // 6
    key_first, key_second, key_flip = jax.random.split(jax.random.fold_in(key, 7), 3)
    shape = (RQ, N_ROW, TC // 2)
    first = jax.random.randint(key_first, shape, lowest, K + 1)
    upper = jnp.minimum(K, RPAIR - first)
    second = jax.random.randint(key_second, shape, lowest, upper + 1)
    row_index = jnp.arange(RQ, dtype=jnp.int32)[:, None, None]
    first = jnp.where(row_index == 0, K, jnp.where(row_index == 1, lowest, first))
    second = jnp.where(row_index == 0, RPAIR - K, second)
    flip = jax.random.randint(key_flip, shape, 0, 2)
    left = jnp.where(flip == 1, second, first)
    right = jnp.where(flip == 1, first, second)
    return jnp.stack([left, right], axis=-1).reshape(RQ, N_ROW, TC).astype(jnp.int32)


def set_ends(result, rng, low, high):
    shape = result.shape
    index_at = [jax.random.randint(jax.random.fold_in(rng, axis), (), 0, shape[axis]) for axis in range(len(shape))]
    result = result.at[tuple(index_at)].set(low)
    longest = shape.index(max(shape))
    index_at[longest] = (index_at[longest] + 1) % shape[longest]
    return result.at[tuple(index_at)].set(high)


def levels(key, extent, shards, smallest, largest):
    loudness = 1.0
    for dim, shards_of in shards:
        steps = jax.random.uniform(jax.random.fold_in(jax.random.fold_in(key, 6), dim), (shards_of,), jnp.float32, smallest / len(shards), largest / len(shards))
        loudness = loudness * jnp.repeat(jnp.exp(steps), extent[dim] // shards_of).reshape((-1,) + (1,) * (len(extent) - 1 - dim))
    return loudness


def centred(key, extent, width, most, shards=(), kind=jnp.bfloat16):
    drawn = width * jax.random.normal(key, extent, jnp.float32)
    if shards:
        drawn = drawn * levels(key, extent, shards, -0.22, 0.18)
    return jnp.clip(drawn, -most, most).astype(kind)


def setup_inputs(seed: int = 0) -> dict:
    streams_of = jax.random.split(jax.random.key(seed), 8)
    latent = centred(streams_of[0], (TC * B, S), 1.0, 6.0, ((0, 64),), jnp.float32)
    v_basis = centred(streams_of[1], (RQ, N_ROW, TC, K, B), B ** -0.5, 0.375, ((1, 4), (2, 64)), jnp.float32)
    u_basis = centred(streams_of[2], (N_COL, N_ROW, B, TC * K), (TC * K) ** -0.5, 0.078125, ((0, 64), (1, 4)), jnp.float32)
    ranks = draw_ranks(jax.random.fold_in(streams_of[7], 71), 0)
    slot_row = jax.vmap(lambda own: jax.random.permutation(own, N_COL))(jax.random.split(streams_of[4], N_ROW)).reshape((N_ROW, N_COL)).astype(jnp.int32)
    wells = set_ends(jax.random.randint(streams_of[5], (N_COL, N_ROW, WPT), 0, B), jax.random.fold_in(streams_of[5], 1), 0, B - 1).astype(jnp.int32)
    observed = jnp.clip(0.3 + 2.2 * jax.random.uniform(streams_of[6], (N_COL, N_ROW, WPT, S), jnp.float32) ** levels(streams_of[6], (N_COL, N_ROW, WPT, S), ((0, 64), (1, 4)), -0.2, 0.2), 0.3, 2.5)
    return {"latent": latent, "v_basis": v_basis, "u_basis": u_basis, "ranks": ranks, "slot_row": slot_row, "wells": wells, "observed": observed}


def reference(latent, v_basis, u_basis, ranks, slot_row, wells, observed):
    highest = lax.Precision.HIGHEST
    latent_tiles = latent.reshape(TC, B, S)
    u_flat = u_basis.reshape(N_COL * N_ROW, B, TC * K)
    wells_flat = wells.reshape(N_COL * N_ROW, WPT)
    observed_flat = observed.reshape(N_COL * N_ROW, WPT, S)
    rank_iota = jnp.arange(K, dtype=jnp.int32)
    cell_iota = jnp.arange(B, dtype=jnp.int32)

    def visit(accumulated, position):
        owner_col = position // N_ROW
        owner_class = position % N_ROW
        tile_row = slot_row[owner_class, owner_col]
        v_rows = v_basis[tile_row, owner_class]
        live_mask = (rank_iota[None, :] < ranks[tile_row, owner_class][:, None]).astype(jnp.float32)
        blocks = jnp.einsum('jkb,jbs->jks', v_rows, latent_tiles, precision=highest) * live_mask[:, :, None]
        u_owned = u_flat[position]
        field_block = jnp.dot(u_owned, blocks.reshape(TC * K, S), precision=highest)
        onehot = (wells_flat[position][:, None] == cell_iota[None, :]).astype(jnp.float32)
        at_wells = jnp.dot(onehot, field_block, precision=highest)
        expo_wells = jnp.exp(at_wells)
        weighted = (expo_wells - observed_flat[position]) * expo_wells / 0.25
        source = jnp.dot(onehot.T, weighted, precision=highest)
        adjoint = jnp.dot(u_owned.T, source, precision=highest).reshape(TC, K, S) * live_mask[:, :, None]
        accumulated = accumulated + jnp.einsum('jkb,jks->jbs', v_rows, adjoint, precision=highest)
        return accumulated, field_block

    accumulated, fields = lax.scan(visit, jnp.zeros((TC, B, S), jnp.float32),
                                   jnp.arange(N_COL * N_ROW, dtype=jnp.int32))
    gradient = latent + accumulated.reshape(TC * B, S)
    return fields.reshape(N_COL, N_ROW, B, S), gradient
```

```python
import jax
import jax.numpy as jnp
from jax import lax
from jax.experimental import pallas as pl
from jax.experimental.pallas import tpu as pltpu
from jax.sharding import PartitionSpec as P

MESH = pl.DeviceIdType.MESH
F32, BF16 = jnp.float32, jnp.bfloat16
K = 48
RPAIR = 72
MID = RPAIR - K
S = 128
B = 256
NC = 64
NR = 4
GS = 4
NG = NC // GS
GB = 8
NGB = NC // GB


def split(x):
    hi = x.astype(BF16)
    return hi, (x - hi.astype(F32)).astype(BF16)


def dot(a, b):
    return jnp.dot(a, b, preferred_element_type=F32)


def flipped(x):
    v = x.reshape(K // 8, 8, S)
    i = lax.broadcasted_iota(jnp.int32, (K // 8, 8, S), 1)
    for step in (1, 2, 4):
        v = jnp.where((i & step) == 0, pltpu.roll(v, 8 - step, 1), pltpu.roll(v, step, 1))
    return jnp.concatenate([v[K // 8 - 1 - t] for t in range(K // 8)], 0)


def pack(a, b):
    r = flipped(b)
    return jnp.concatenate([a[:MID], a[MID:] + r[:MID], r[MID:]], 0)


def kernel(
    slot_s, ranks_s, wells_s, lat, obs, v_hbm, u_hbm, field_o, grad_o,
    v, u, l2, u2, ur, wt, vt, sbuf, rbuf, sbuf2, rbuf2, rrs, rrr, atw, gacc, xrecv,
    vsem, usem, lsem, ssem, rsem, rrssem, rrrsem, ssem2, rsem2, xssem, xrsem,
):
    me = lax.axis_index("col")
    row = lax.axis_index("row")
    mg = me // GS
    mu = me % GS
    vcopy = pltpu.make_async_copy(v_hbm, v, vsem)
    vcopy.start()
    ucopy = pltpu.make_async_copy(u_hbm, u, usem)
    ucopy.start()

    barrier = pltpu.get_barrier_semaphore()

    def greet(i, c):
        pl.semaphore_signal(barrier, inc=1, device_id=((me + i) % NC, row), device_id_type=MESH)
        return c

    lax.fori_loop(1, NC, greet, 0)
    for i in range(1, NR):
        pl.semaphore_signal(barrier, inc=1, device_id=(me, (row + i) % NR), device_id_type=MESH)

    rows48 = lax.broadcasted_iota(jnp.int32, (K, S), 0)
    rows48f = rows48.astype(F32)

    lhi, llo = split(lat[...])
    l2[:, :S] = lhi
    l2[:, S:] = llo

    def peer(k, i):
        return GS * ((mg + k) % NG) + (i + mu) % GS

    def rank_row(k, c):
        for i in range(GS):
            q = slot_s[peer(k, i)]
            first = lax.broadcasted_iota(jnp.int32, (2, S), 0) == 0
            rrs[GS * k + i] = jnp.where(first, ranks_s[q, 0], ranks_s[q, 1]).astype(F32)
        return c

    lax.fori_loop(0, NG, rank_row, 0)
    rrr[me] = rrs[0]
    vcopy.wait()

    def products(x, half):
        hi, lo = split(x)
        n = x.shape[0]
        p = dot(jnp.concatenate([hi, lo], 0), l2[B * half : B * half + B, :])
        return p[:n, :S] + p[:n, S:] + p[n:, :S]

    def forward(k):
        qs = [slot_s[peer(k, i)] for i in range(GS)]
        tiles = [v[q] for q in qs]
        a = products(jnp.concatenate([x[:K] for x in tiles], 0), 0)
        b = products(jnp.concatenate([x[K:] for x in tiles], 0), 1)
        for i in range(GS):
            ai = jnp.where(rows48 < ranks_s[qs[i], 0], a[K * i : K * i + K], 0.0)
            bi = jnp.where(rows48 < ranks_s[qs[i], 1], b[K * i : K * i + K], 0.0)
            sbuf[GS * k + i] = pack(ai, bi)

    def send(src, dst, sems, ss, per, k, i):
        pltpu.make_async_remote_copy(
            src_ref=src.at[GS * k + i],
            dst_ref=dst.at[me],
            send_sem=ss,
            recv_sem=sems.at[me // per],
            device_id=(peer(k, i), row),
            device_id_type=MESH,
        ).start()

    forward(0)
    pl.semaphore_wait(barrier, NC - 1 + NR - 1)

    def send_ranks(k, i):
        pltpu.make_async_remote_copy(
            src_ref=rrs.at[GS * k + i],
            dst_ref=rrr.at[me],
            send_sem=rrssem,
            recv_sem=rrrsem,
            device_id=(peer(k, i), row),
            device_id_type=MESH,
        ).start()

    for i in range(1, GS):
        send_ranks(0, i)

    def ranks_loop(k, c):
        for i in range(GS):
            send_ranks(k, i)
        return c

    lax.fori_loop(1, NG, ranks_loop, 0)

    forward(1)
    own = pltpu.make_async_copy(sbuf.at[0], rbuf.at[me], lsem)
    own.start()
    for i in range(1, GS):
        send(sbuf, rbuf, rsem, ssem, GS, 0, i)

    def forward_loop(k, c):
        forward(k)
        for i in range(GS):
            send(sbuf, rbuf, rsem, ssem, GS, k - 1, i)
        return c

    lax.fori_loop(2, NG, forward_loop, 0)
    for i in range(GS):
        send(sbuf, rbuf, rsem, ssem, GS, NG - 1, i)

    ucopy.wait()

    def split_u(c, carry):
        at = pl.ds(pl.multiple_of(512 * c, 512), 512)
        hi, lo = split(u[:, at])
        u2[0, :, at] = hi
        u2[1, :, at] = lo
        return carry

    lax.fori_loop(0, NC * 2 * K // 512, split_u, 0)

    def well_row(w, c):
        ur[pl.ds(w, 1), :] = u[pl.ds(wells_s[w], 1), :]
        return c

    lax.fori_loop(0, 64, well_row, 0)

    def well_block(c, carry):
        at = pl.ds(pl.multiple_of(S * c, S), S)
        x = ur[:, at]
        hi = x.astype(BF16).astype(F32)
        wt[at, :] = jnp.concatenate([hi, x - hi], 0).T.astype(BF16)
        return carry

    lax.fori_loop(0, NC * 2 * K // S, well_block, 0)

    def basis_block(g, carry):
        at = pl.ds(pl.multiple_of(GB * K * g, S), GB * K)
        tiles = [v[slot_s[GB * g + j]] for j in range(GB)]
        for half in range(2):
            x = jnp.concatenate([t[K * half : K * half + K] for t in tiles], 0).T
            hi, lo = split(x)
            vt[0, half, :, at] = hi
            vt[1, half, :, at] = lo
        return carry

    lax.fori_loop(0, NGB, basis_block, 0)

    pltpu.make_async_copy(rrr.at[pl.ds(0, NC - 1)], rrr.at[pl.ds(0, NC - 1)], rrrsem).wait()
    field_o[...] = jnp.zeros_like(field_o)

    def unpacked(packed, r1, r2):
        a = jnp.where(rows48f < r1, packed[:K], 0.0)
        b = jnp.where(rows48f < r2, flipped(packed[MID:]), 0.0)
        return a, b

    def field_group(g):
        parts = []
        for i in range(GS):
            s = GS * g + i
            rr = rrr[s]
            parts += unpacked(rbuf[s], rr[0:1], rr[1:2])
        hi, lo = split(jnp.concatenate(parts, 0))
        at = pl.ds(pl.multiple_of(GS * 2 * K * g, S), GS * 2 * K)
        p = dot(u2[0, :, at], jnp.concatenate([hi, lo], 1))
        q = dot(u2[1, :, at], hi)
        field_o[...] += p[:, :S] + p[:, S:] + q

    def wait_for(buf, sem, n):
        pltpu.make_async_copy(buf.at[pl.ds(0, n)], buf.at[pl.ds(0, n)], sem).wait()

    def field_loop(k, c):
        g = (mg - k + NG) % NG
        wait_for(rbuf, rsem.at[g], GS)
        field_group(g)
        return c

    lax.fori_loop(1, NG, field_loop, 0)
    own.wait()
    wait_for(rbuf, rsem.at[mg], GS - 1)
    field_group(mg)

    def at_well(w, c):
        atw[pl.ds(w, 1), :] = field_o[pl.ds(wells_s[w], 1), :]
        return c

    lax.fori_loop(0, 64, at_well, 0)
    e = jnp.exp(atw[...])
    whi, wlo = split((e - obs[...]) * e / 0.25)
    zero = jnp.zeros_like(whi)
    wr = jnp.concatenate(
        [jnp.concatenate([whi, wlo], 1), jnp.concatenate([whi, zero], 1)], 0
    )

    def backward(k):
        g = (mg + k) % NG
        at = pl.ds(pl.multiple_of(GS * 2 * K * g, S), GS * 2 * K)
        p = dot(wt[at, :], wr)
        return g, p[:, :S] + p[:, S:]

    gacc[...] = jnp.zeros_like(gacc)

    def backward_group(k):
        g, x = backward(k)
        for i in range(GS):
            s = GS * g + i
            rr = rrr[s]
            a = jnp.where(rows48f < rr[0:1], x[2 * K * i : 2 * K * i + K], 0.0)
            b = jnp.where(rows48f < rr[1:2], x[2 * K * i + K : 2 * K * i + 2 * K], 0.0)
            sbuf2[GS * k + (i - mu + GS) % GS] = pack(a, b)

    backward_group(0)
    backward_group(1)
    own2 = pltpu.make_async_copy(sbuf2.at[0], rbuf2.at[me], lsem)
    own2.start()
    for i in range(1, GS):
        send(sbuf2, rbuf2, rsem2, ssem2, GB, 0, i)

    def backward_loop(k, c):
        backward_group(k)
        for i in range(GS):
            send(sbuf2, rbuf2, rsem2, ssem2, GB, k - 1, i)
        return c

    lax.fori_loop(2, NG, backward_loop, 0)
    for i in range(GS):
        send(sbuf2, rbuf2, rsem2, ssem2, GB, NG - 1, i)

    mb = me // GB

    def gradient_group(g):
        pa, pb = [], []
        for j in range(GB):
            c = GB * g + j
            q = slot_s[c]
            packed = rbuf2[c]
            pa.append(jnp.where(rows48 < ranks_s[q, 0], packed[:K], 0.0))
            pb.append(jnp.where(rows48 < ranks_s[q, 1], flipped(packed[MID:]), 0.0))
        at = pl.ds(pl.multiple_of(GB * K * g, S), GB * K)
        for half, parts in ((0, pa), (1, pb)):
            hi, lo = split(jnp.concatenate(parts, 0))
            p = dot(vt[0, half, :, at], jnp.concatenate([hi, lo], 1))
            q = dot(vt[1, half, :, at], hi)
            gacc[B * half : B * half + B, :] += p[:, :S] + p[:, S:] + q

    def gradient_loop(k, c):
        g = (mb - k + NGB) % NGB
        wait_for(rbuf2, rsem2.at[g], GB)
        gradient_group(g)
        return c

    lax.fori_loop(1, NGB, gradient_loop, 0)
    own2.wait()
    wait_for(rbuf2, rsem2.at[mb], GB - 1)
    gradient_group(mb)

    part = 2 * B // NR

    def exchange(d):
        to = (row + d) % NR
        return pltpu.make_async_remote_copy(
            src_ref=gacc.at[pl.ds(pl.multiple_of(part * to, part), part)],
            dst_ref=xrecv.at[d - 1],
            send_sem=xssem.at[d - 1],
            recv_sem=xrsem.at[d - 1],
            device_id=(me, to),
            device_id_type=MESH,
        )

    moves = [exchange(d) for d in range(1, NR)]
    for m in moves:
        m.start()
    mine = pl.ds(pl.multiple_of(part * row, part), part)
    total = lat[mine, :] + gacc[mine, :]
    for d in range(1, NR):
        moves[d - 1].wait_recv()
        total += xrecv[d - 1]
    grad_o[...] = total
    for m in moves:
        m.wait_send()
    wait_for(sbuf, ssem, NC - 1)
    wait_for(sbuf2, ssem2, NC - 1)
    wait_for(rrs, rrssem, NC - 1)


def on_device(latent, v_basis, u_basis, ranks, slot_row, wells, observed):
    vmem = pl.BlockSpec(memory_space=pltpu.VMEM)
    smem = pl.BlockSpec(memory_space=pltpu.SMEM)
    anywhere = pl.BlockSpec(memory_space=pl.ANY)
    dma = pltpu.SemaphoreType.DMA
    field, gradient = pl.pallas_call(
        kernel,
        name="tlr",
        out_shape=(
            jax.ShapeDtypeStruct((B, S), F32),
            jax.ShapeDtypeStruct((2 * B // NR, S), F32),
        ),
        in_specs=[smem, smem, smem, vmem, vmem, anywhere, anywhere],
        out_specs=(vmem, vmem),
        scratch_shapes=[
            pltpu.VMEM((NC, 2 * K, B), F32),
            pltpu.VMEM((B, NC * 2 * K), F32),
            pltpu.VMEM((2 * B, 2 * S), BF16),
            pltpu.VMEM((2, B, NC * 2 * K), BF16),
            pltpu.VMEM((64, NC * 2 * K), F32),
            pltpu.VMEM((NC * 2 * K, S), BF16),
            pltpu.VMEM((2, 2, B, NC * K), BF16),
            pltpu.VMEM((NC, RPAIR, S), F32),
            pltpu.VMEM((NC, RPAIR, S), F32),
            pltpu.VMEM((NC, RPAIR, S), F32),
            pltpu.VMEM((NC, RPAIR, S), F32),
            pltpu.VMEM((NC, 2, S), F32),
            pltpu.VMEM((NC, 2, S), F32),
            pltpu.VMEM((64, S), F32),
            pltpu.VMEM((2 * B, S), F32),
            pltpu.VMEM((NR - 1, 2 * B // NR, S), F32),
            dma, dma, dma, dma, dma((NG,)), dma, dma, dma, dma((NGB,)),
            dma((NR - 1,)), dma((NR - 1,)),
        ],
        compiler_params=pltpu.CompilerParams(
            collective_id=0, has_side_effects=True, vmem_limit_bytes=60 * 2**20
        ),
    )(
        slot_row[0],
        ranks[:, 0],
        wells[0, 0],
        latent,
        observed[0, 0],
        v_basis.reshape(NC, 2 * K, B),
        u_basis[0, 0],
    )
    return (field[None, None], gradient)


def solution(mesh):
    placed = (
        P("col", None),
        P(None, "row", "col", None, None),
        P("col", "row", None, None),
        P(None, "row", "col"),
        P("row", None),
        P("col", "row", None),
        P("col", "row", None, None),
    )
    return jax.shard_map(
        on_device,
        mesh=mesh,
        in_specs=placed,
        out_specs=(P("col", "row", None, None), P(("col", "row"), None)),
        check_vma=False,
    )
```

```python
import jax
import jax.numpy as jnp
from jax import lax
from jax.experimental import pallas as pl
from jax.experimental.pallas import tpu as pltpu
from jax.sharding import PartitionSpec as P

MESH = pl.DeviceIdType.MESH
F32, BF16 = jnp.float32, jnp.bfloat16
K = 48
RPAIR = 72
MID = RPAIR - K
S = 128
B = 256
NC = 64
NR = 4
GS = 4
NG = NC // GS
GB = 8
NGB = NC // GB
NY = 4
NZ = 8
WPT = 64
HALF = 40
EARLY = 21


def split(x):
    hi = x.astype(BF16)
    return hi, (x - hi.astype(F32)).astype(BF16)


def dot(a, b):
    return jnp.dot(a, b, preferred_element_type=F32)


def flipped(x):
    v = x.reshape(K // 8, 8, S)
    i = lax.broadcasted_iota(jnp.int32, (K // 8, 8, S), 1)
    for step in (1, 2, 4):
        v = jnp.where((i & step) == 0, pltpu.roll(v, 8 - step, 1), pltpu.roll(v, step, 1))
    return jnp.concatenate([v[K // 8 - 1 - t] for t in range(K // 8)], 0)


def pack(a, b):
    r = flipped(b)
    return jnp.concatenate([a[:MID], a[MID:] + r[:MID], r[MID:]], 0)


def kernel(
    slot_s, ranks_s, wells_s, lat, obs, v_hbm, u_hbm, field_o, grad_o,
    v, u, l2, u2, ur, ut, vt, sbuf, rbuf, sbuf2, rbuf2, rrs, rrr, wag, gacc, xrecv,
    vsem, usem, lsem, lsem2, ssem, rsem, rrssem, rrrsem, ssem2, rsem2, zssem, zrsem, yssem, yrsem, pssem, prsem, xssem, xrsem,
):
    me = lax.axis_index("col")
    row = lax.axis_index("row")
    mg = me // GS
    mu = me % GS
    my = me // (NZ * 2)
    mz = me // 2 % NZ
    mc = me % 2
    vcopy = pltpu.make_async_copy(v_hbm, v, vsem)
    vcopy.start()
    ucopy = pltpu.make_async_copy(u_hbm, u, usem)
    ucopy.start()

    barrier = pltpu.get_barrier_semaphore()

    def greet(i, c):
        pl.semaphore_signal(barrier, inc=1, device_id=((me + i) % NC, row), device_id_type=MESH)
        return c

    lax.fori_loop(1, NC, greet, 0)
    for i in range(1, NR):
        pl.semaphore_signal(barrier, inc=1, device_id=(me, (row + i) % NR), device_id_type=MESH)

    rows48 = lax.broadcasted_iota(jnp.int32, (K, S), 0)
    rows48f = rows48.astype(F32)

    lhi, llo = split(lat[...])
    l2[:, :S] = lhi
    l2[:, S:] = llo

    def peer(k, i):
        return GS * ((mg + k) % NG) + (i + mu) % GS

    def copy_to(src, dst, ss, rs, col):
        return pltpu.make_async_remote_copy(
            src_ref=src,
            dst_ref=dst,
            send_sem=ss,
            recv_sem=rs,
            device_id=(col, row),
            device_id_type=MESH,
        )

    def wait_for(buf, sem, n):
        pltpu.make_async_copy(buf.at[pl.ds(0, n)], buf.at[pl.ds(0, n)], sem).wait()

    def rank_row(k, c):
        for i in range(GS):
            q = slot_s[peer(k, i)]
            first = lax.broadcasted_iota(jnp.int32, (2, S), 0) == 0
            rrs[GS * k + i] = jnp.where(first, ranks_s[0, q], ranks_s[1, q]).astype(F32)
        return c

    lax.fori_loop(0, NG, rank_row, 0)
    rrr[me] = rrs[0]
    vcopy.wait()

    def products(x, half):
        hi, lo = split(x)
        n = x.shape[0]
        p = dot(jnp.concatenate([hi, lo], 0), l2[B * half : B * half + B, :])
        return p[:n, :S] + p[:n, S:] + p[n:, :S]

    def forward(k):
        qs = [slot_s[peer(k, i)] for i in range(GS)]
        tiles = [v[q] for q in qs]
        a = products(jnp.concatenate([x[:K] for x in tiles], 0), 0)
        b = products(jnp.concatenate([x[K:] for x in tiles], 0), 1)
        for i in range(GS):
            ai = jnp.where(rows48 < ranks_s[0, qs[i]], a[K * i : K * i + K], 0.0)
            bi = jnp.where(rows48 < ranks_s[1, qs[i]], b[K * i : K * i + K], 0.0)
            sbuf[GS * k + i] = pack(ai, bi)

    def send(k, i):
        copy_to(sbuf.at[GS * k + i], rbuf.at[me], ssem, rsem.at[mg], peer(k, i)).start()

    def send_ranks(k, i):
        copy_to(rrs.at[GS * k + i], rrr.at[me], rrssem, rrrsem, peer(k, i)).start()

    forward(0)
    pl.semaphore_wait(barrier, NC - 1 + NR - 1)
    for i in range(1, GS):
        send_ranks(0, i)

    def ranks_loop(k, c):
        for i in range(GS):
            send_ranks(k, i)
        return c

    lax.fori_loop(1, NG, ranks_loop, 0)

    forward(1)
    own = pltpu.make_async_copy(sbuf.at[0], rbuf.at[me], lsem)
    own.start()
    for i in range(1, GS):
        send(0, i)

    def forward_loop(k, c):
        forward(k)
        for i in range(GS):
            send(k - 1, i)
        return c

    lax.fori_loop(2, NG, forward_loop, 0)
    for i in range(GS):
        send(NG - 1, i)

    ucopy.wait()

    def well_row(w, c):
        at = u[pl.ds(wells_s[w], 1), :]
        ur[pl.ds(w, 1), :] = at
        ur[pl.ds(w + WPT, 1), :] = at
        return c

    lax.fori_loop(0, WPT, well_row, 0)

    def well_block(c, carry):
        at = pl.ds(pl.multiple_of(S * c, S), S)
        ut[at, :] = ur[:, at].T
        return carry

    lax.fori_loop(0, NC * 2 * K // S, well_block, 0)
    wait_for(rrr, rrrsem, NC - 1)
    left = lax.broadcasted_iota(jnp.int32, (HALF, S), 1) < WPT

    def pack_wells(j, carry):
        rr = rrr[j]
        x = ut[pl.ds(pl.multiple_of(2 * K * j, 2 * K), 2 * K), :]
        p = pack(
            jnp.where(rows48f < rr[0:1], x[:K], 0.0),
            jnp.where(rows48f < rr[1:2], x[K:], 0.0),
        )
        tail = jnp.concatenate([p[HALF:], jnp.zeros((2 * HALF - RPAIR, S), F32)], 0)
        sbuf2[j] = jnp.where(left, p[:HALF], tail)
        return carry

    lax.fori_loop(0, NC, pack_wells, 0)
    own2 = pltpu.make_async_copy(sbuf2.at[me], rbuf2.at[me], lsem2)
    own2.start()

    def send_wells(n):
        to = 16 * ((my + n // 16) % NY) + (me + n) % 16
        copy_to(sbuf2.at[to], rbuf2.at[me], ssem2, rsem2.at[me // GB], to).start()

    def send_wells_from(start, n):
        def one(i, c):
            send_wells(start + i)
            return c

        lax.fori_loop(0, n, one, 0)

    send_wells_from(1, EARLY)

    def split_u(c, carry):
        at = pl.ds(pl.multiple_of(512 * c, 512), 512)
        hi, lo = split(u[:, at])
        u2[0, :, at] = hi
        u2[1, :, at] = lo
        return carry

    lax.fori_loop(0, NC * 2 * K // 512, split_u, 0)

    def basis_block(g, carry):
        at = pl.ds(pl.multiple_of(GB * K * g, S), GB * K)
        tiles = [v[slot_s[GB * g + j]] for j in range(GB)]
        for half in range(2):
            x = jnp.concatenate([t[K * half : K * half + K] for t in tiles], 0).T
            hi, lo = split(x)
            vt[0, half, :, at] = hi
            vt[1, half, :, at] = lo
        return carry

    lax.fori_loop(0, NGB, basis_block, 0)

    field_o[...] = jnp.zeros_like(field_o)

    def field_group(g):
        parts = []
        for i in range(GS):
            s = GS * g + i
            rr = rrr[s]
            x = rbuf[s]
            parts.append(jnp.where(rows48f < rr[0:1], x[:K], 0.0))
            parts.append(jnp.where(rows48f < rr[1:2], flipped(x[MID:]), 0.0))
        hi, lo = split(jnp.concatenate(parts, 0))
        at = pl.ds(pl.multiple_of(GS * 2 * K * g, S), GS * 2 * K)
        p = dot(u2[0, :, at], jnp.concatenate([hi, lo], 1))
        q = dot(u2[1, :, at], hi)
        field_o[...] += p[:, :S] + p[:, S:] + q

    def field_loop(k, c):
        g = (mg - k + NG) % NG
        wait_for(rbuf, rsem.at[g], GS)
        field_group(g)
        return c

    lax.fori_loop(1, NG, field_loop, 0)
    own.wait()
    wait_for(rbuf, rsem.at[mg], GS - 1)
    field_group(mg)

    def at_well(w, c):
        gacc[pl.ds(w, 1), :] = field_o[pl.ds(wells_s[w], 1), :]
        return c

    lax.fori_loop(0, WPT, at_well, 0)
    e = jnp.exp(gacc[:WPT])
    wag[me] = (e - obs[...]) * e / 0.25
    gacc[...] = jnp.zeros_like(gacc)

    def col(y, z, c):
        return (y % NY) * (NZ * 2) + (z % NZ) * 2 + c

    partner = me + 1 - 2 * mc
    for d in (4, 3, 5, 2, 6, 1, 7):
        copy_to(wag.at[me], wag.at[me], zssem, zrsem.at[d], col(my, mz + d, mc)).start()

    def to_partner(s, dy):
        copy_to(wag.at[s], wag.at[s], pssem, prsem.at[dy], partner).start()

    def relay(s, z):
        for dy in range(1, NY):
            copy_to(wag.at[s], wag.at[s], yssem, yrsem.at[dy * NZ + z], col(my + dy, mz, mc)).start()
        to_partner(s, 0)

    relay(me, mz)
    rest = NC - 1 - EARLY
    done = 0
    for n, d in enumerate((1, 7, 2, 6, 3, 5, 4)):
        upto = rest * (n + 1) // 7
        send_wells_from(1 + EARLY + done, upto - done)
        done = upto
        s = col(my, mz + NZ - d, mc)
        wait_for(wag, zrsem.at[d], 1)
        relay(s, (mz + NZ - d) % NZ)

    left80 = lax.broadcasted_iota(jnp.int32, (HALF, S), 1) < WPT

    def gradient_group(g):
        pa, pb = [], []
        for j in range(GB):
            c = GB * g + j
            q = slot_s[c]
            m = rbuf2[c]
            hi = m.astype(BF16).astype(F32)
            lo = m - hi
            rows = jnp.concatenate(
                [
                    jnp.where(left80, hi, pltpu.roll(lo, WPT, 1)),
                    jnp.where(left80, pltpu.roll(hi, WPT, 1), lo),
                ],
                0,
            ).astype(BF16)
            whi, wlo = split(wag[c])
            w2 = jnp.concatenate(
                [
                    jnp.concatenate([whi, wlo], 1),
                    jnp.concatenate([whi, jnp.zeros_like(whi)], 1),
                ],
                0,
            )
            p = dot(rows, w2)
            adj = p[:, :S] + p[:, S:]
            pa.append(jnp.where(rows48 < ranks_s[0, q], adj[:K], 0.0))
            pb.append(jnp.where(rows48 < ranks_s[1, q], flipped(adj[MID:RPAIR]), 0.0))
        at = pl.ds(pl.multiple_of(GB * K * g, S), GB * K)
        for half, parts in ((0, pa), (1, pb)):
            hi, lo = split(jnp.concatenate(parts, 0))
            p = dot(vt[0, half, :, at], jnp.concatenate([hi, lo], 1))
            q = dot(vt[1, half, :, at], hi)
            gacc[B * half : B * half + B, :] += p[:, :S] + p[:, S:] + q

    def line(dy):
        y = (my - dy + NY) % NY
        wait_for(wag, prsem.at[dy], NZ)

        def half_line(h, c):
            g = 2 * y + h
            wait_for(rbuf2, rsem2.at[g], GB)
            gradient_group(g)
            return c

        lax.fori_loop(0, 2, half_line, 0)

    def pass_on(dy):
        def one(z, c):
            wait_for(wag, yrsem.at[dy * NZ + z], 1)
            to_partner(col(my + NY - dy, z, mc), dy)
            return c

        lax.fori_loop(0, NZ, one, 0)

    pass_on(1)
    wait_for(wag, prsem.at[0], NZ)
    own2.wait()
    wait_for(rbuf2, rsem2.at[me // GB], GB - 1)
    gradient_group(me // GB)
    other = 2 * my + 1 - me // GB % 2
    wait_for(rbuf2, rsem2.at[other], GB)
    gradient_group(other)
    pass_on(2)
    line(1)
    pass_on(3)
    line(2)
    line(3)

    part = 2 * B // NR

    def exchange(d):
        to = (row + d) % NR
        return pltpu.make_async_remote_copy(
            src_ref=gacc.at[pl.ds(pl.multiple_of(part * to, part), part)],
            dst_ref=xrecv.at[d - 1],
            send_sem=xssem.at[d - 1],
            recv_sem=xrsem.at[d - 1],
            device_id=(me, to),
            device_id_type=MESH,
        )

    moves = [exchange(d) for d in range(1, NR)]
    for m in moves:
        m.start()
    mine = pl.ds(pl.multiple_of(part * row, part), part)
    total = lat[mine, :] + gacc[mine, :]
    for d in range(1, NR):
        moves[d - 1].wait_recv()
        total += xrecv[d - 1]
    grad_o[...] = total
    for m in moves:
        m.wait_send()
    wait_for(sbuf, ssem, NC - 1)
    wait_for(sbuf2, ssem2, NC - 1)
    wait_for(rrs, rrssem, NC - 1)
    wait_for(wag, zssem, NZ - 1)
    wait_for(wag, yssem, NZ * (NY - 1))
    wait_for(wag, pssem, NZ * NY)


def on_device(latent, v_basis, u_basis, ranks, slot_row, wells, observed):
    vmem = pl.BlockSpec(memory_space=pltpu.VMEM)
    smem = pl.BlockSpec(memory_space=pltpu.SMEM)
    anywhere = pl.BlockSpec(memory_space=pl.ANY)
    dma = pltpu.SemaphoreType.DMA
    field, gradient = pl.pallas_call(
        kernel,
        name="tlr",
        out_shape=(
            jax.ShapeDtypeStruct((B, S), F32),
            jax.ShapeDtypeStruct((2 * B // NR, S), F32),
        ),
        in_specs=[smem, smem, smem, vmem, vmem, anywhere, anywhere],
        out_specs=(vmem, vmem),
        scratch_shapes=[
            pltpu.VMEM((NC, 2 * K, B), F32),
            pltpu.VMEM((B, NC * 2 * K), F32),
            pltpu.VMEM((2 * B, 2 * S), BF16),
            pltpu.VMEM((2, B, NC * 2 * K), BF16),
            pltpu.VMEM((2 * WPT, NC * 2 * K), F32),
            pltpu.VMEM((NC * 2 * K, S), F32),
            pltpu.VMEM((2, 2, B, NC * K), BF16),
            pltpu.VMEM((NC, RPAIR, S), F32),
            pltpu.VMEM((NC, RPAIR, S), F32),
            pltpu.VMEM((NC, HALF, S), F32),
            pltpu.VMEM((NC, HALF, S), F32),
            pltpu.VMEM((NC, 2, S), F32),
            pltpu.VMEM((NC, 2, S), F32),
            pltpu.VMEM((NC, WPT, S), F32),
            pltpu.VMEM((2 * B, S), F32),
            pltpu.VMEM((NR - 1, 2 * B // NR, S), F32),
            dma, dma, dma, dma, dma, dma((NG,)), dma, dma, dma, dma((NGB,)),
            dma, dma((NZ,)), dma, dma((NY * NZ,)), dma, dma((NY,)),
            dma((NR - 1,)), dma((NR - 1,)),
        ],
        compiler_params=pltpu.CompilerParams(
            collective_id=0, has_side_effects=True, vmem_limit_bytes=60 * 2**20
        ),
    )(
        slot_row[0],
        ranks[:, 0].T,
        wells[0, 0],
        latent,
        observed[0, 0],
        v_basis.reshape(NC, 2 * K, B),
        u_basis[0, 0],
    )
    return (field[None, None], gradient)


def solution(mesh):
    placed = (
        P("col", None),
        P(None, "row", "col", None, None),
        P("col", "row", None, None),
        P(None, "row", "col"),
        P("row", None),
        P("col", "row", None),
        P("col", "row", None, None),
    )
    return jax.shard_map(
        on_device,
        mesh=mesh,
        in_specs=placed,
        out_specs=(P("col", "row", None, None), P(("col", "row"), None)),
        check_vma=False,
    )
```

```python
import jax
import jax.numpy as jnp
from jax import lax
from jax.experimental import pallas as pl
from jax.experimental.pallas import tpu as pltpu
from jax.sharding import PartitionSpec as P

MESH = pl.DeviceIdType.MESH
F32, BF16 = jnp.float32, jnp.bfloat16
K = 48
RPAIR = 72
MID = RPAIR - K
S = 128
B = 256
NC = 64
NR = 4
GS = 4
NG = NC // GS
GB = 8
NGB = NC // GB
NY = 4
NZ = 8
WPT = 64
HALF = 40
TOP = 32
EARLY = 12
PACE = 8
LAG = 6
ORDER = [GB * g + n for g in (7, 6, 0, 1, 2, 3, 4, 5) for n in range(GB)]
OTHER = (0, 2, 1, 4, 3, 6, 5, 7)


def split(x):
    hi = x.astype(BF16)
    return hi, (x - hi.astype(F32)).astype(BF16)


def dot(a, b):
    return jnp.dot(a, b, preferred_element_type=F32)


def flipped(x):
    v = x.reshape(K // 8, 8, S)
    i = lax.broadcasted_iota(jnp.int32, (K // 8, 8, S), 1)
    for step in (1, 2, 4):
        v = jnp.where((i & step) == 0, pltpu.roll(v, 8 - step, 1), pltpu.roll(v, step, 1))
    return jnp.concatenate([v[K // 8 - 1 - t] for t in range(K // 8)], 0)


def pack(a, b):
    r = flipped(b)
    return jnp.concatenate([a[:MID], a[MID:] + r[:MID], r[MID:]], 0)


def kernel(
    slot_s, ranks_s, wells_s, lat, obs, v_hbm, u_hbm, field_o, grad_o,
    v, u, l2, u2, ur, ut, vt, sbuf, rbuf, sbuf2, rbuf2, rrs, rrr, wag, gacc, xrecv,
    vsem, usem, lsem, lsem2, ssem, rsem, rrssem, rrrsem, ssem2, rsem2, agsem, zrsem, yrsem, prsem, source_s, xssem, xrsem,
):
    me = lax.axis_index("col")
    row = lax.axis_index("row")
    mg = me // GS
    mu = me % GS
    my = me // (NZ * 2)
    mz = me // 2 % NZ
    mc = me % 2
    vcopy = pltpu.make_async_copy(v_hbm, v, vsem)
    vcopy.start()
    ucopy = pltpu.make_async_copy(u_hbm, u, usem)

    barrier = pltpu.get_barrier_semaphore()

    def greet(i, c):
        pl.semaphore_signal(barrier, inc=1, device_id=((me + i) % NC, row), device_id_type=MESH)
        return c

    lax.fori_loop(1, NC, greet, 0)
    for i in range(1, NR):
        pl.semaphore_signal(barrier, inc=1, device_id=(me, (row + i) % NR), device_id_type=MESH)

    rows48 = lax.broadcasted_iota(jnp.int32, (K, S), 0)
    rows48f = rows48.astype(F32)

    lhi, llo = split(lat[...])
    l2[:, :S] = lhi
    l2[:, S:] = llo

    def peer(k, i):
        return GS * ((mg + k) % NG) + (i + mu) % GS

    def copy_to(src, dst, ss, rs, col):
        return pltpu.make_async_remote_copy(
            src_ref=src,
            dst_ref=dst,
            send_sem=ss,
            recv_sem=rs,
            device_id=(col, row),
            device_id_type=MESH,
        )

    def wait_for(buf, sem, n):
        pltpu.make_async_copy(buf.at[pl.ds(0, n)], buf.at[pl.ds(0, n)], sem).wait()

    def rank_row(k, c):
        for i in range(GS):
            q = slot_s[peer(k, i)]
            first = lax.broadcasted_iota(jnp.int32, (2, S), 0) == 0
            rrs[GS * k + i] = jnp.where(first, ranks_s[0, q], ranks_s[1, q]).astype(F32)
        return c

    lax.fori_loop(0, NG, rank_row, 0)
    rrr[me] = rrs[0]

    def col(y, z, c):
        return y % NY * (NZ * 2) + z % NZ * 2 + c % 2

    ahead = 1 - 2 * mc

    def steps_z(i):
        return (ahead if i % 2 else -ahead) * ((i + 1) // 2)

    for i in range(NGB):
        for n in range(GB):
            source_s[GB * i + n] = col(my + NY - n // 2, mz + NZ - steps_z(i), mc + n)

    vcopy.wait()
    ucopy.start()

    def products(x, half):
        hi, lo = split(x)
        n = x.shape[0]
        p = dot(jnp.concatenate([hi, lo], 0), l2[B * half : B * half + B, :])
        return p[:n, :S] + p[:n, S:] + p[n:, :S]

    def forward(k):
        qs = [slot_s[peer(k, i)] for i in range(GS)]
        tiles = [v[q] for q in qs]
        a = products(jnp.concatenate([x[:K] for x in tiles], 0), 0)
        b = products(jnp.concatenate([x[K:] for x in tiles], 0), 1)
        for i in range(GS):
            ai = jnp.where(rows48 < ranks_s[0, qs[i]], a[K * i : K * i + K], 0.0)
            bi = jnp.where(rows48 < ranks_s[1, qs[i]], b[K * i : K * i + K], 0.0)
            sbuf[GS * k + i] = pack(ai, bi)

    def send(k, i):
        copy_to(sbuf.at[GS * k + i], rbuf.at[me], ssem, rsem.at[mg], peer(k, i)).start()

    def send_ranks(k, i):
        copy_to(rrs.at[GS * k + i], rrr.at[me], rrssem, rrrsem, peer(k, i)).start()

    forward(0)
    pl.semaphore_wait(barrier, NC - 1 + NR - 1)
    for i in range(1, GS):
        send_ranks(0, i)

    def ranks_loop(k, c):
        for i in range(GS):
            send_ranks(k, i)
        return c

    lax.fori_loop(1, NG, ranks_loop, 0)

    forward(1)
    own = pltpu.make_async_copy(sbuf.at[0], rbuf.at[me], lsem)
    own.start()
    for i in range(1, GS):
        send(0, i)

    def forward_loop(k, c):
        forward(k)
        for i in range(GS):
            send(k - 1, i)
        return c

    lax.fori_loop(2, NG, forward_loop, 0)
    for i in range(GS):
        send(NG - 1, i)

    ucopy.wait()

    def well_row(w, c):
        at = u[pl.ds(wells_s[w], 1), :]
        ur[pl.ds(w, 1), :] = at
        ur[pl.ds(w + WPT, 1), :] = at
        return c

    lax.fori_loop(0, WPT, well_row, 0)

    def well_block(c, carry):
        at = pl.ds(pl.multiple_of(S * c, S), S)
        ut[at, :] = ur[:, at].T
        return carry

    lax.fori_loop(0, NC * 2 * K // S, well_block, 0)
    wait_for(rrr, rrrsem, NC - 1)
    left = lax.broadcasted_iota(jnp.int32, (TOP, S), 1) < WPT
    left8 = lax.broadcasted_iota(jnp.int32, (8, S), 1) < WPT
    upper8 = lax.broadcasted_iota(jnp.int32, (8, S), 0) < 4

    def pack_wells(j, carry):
        rr = rrr[j]
        x = ut[pl.ds(pl.multiple_of(2 * K * j, 2 * K), 2 * K), :]
        p = pack(
            jnp.where(rows48f < rr[0:1], x[:K], 0.0),
            jnp.where(rows48f < rr[1:2], x[K:], 0.0),
        )
        sbuf2[j, :TOP] = jnp.where(left, p[:TOP], p[TOP : 2 * TOP])
        end = p[2 * TOP :]
        sbuf2[j, TOP:] = jnp.where(left8, end, pltpu.roll(end, 4, 0))
        return carry

    lax.fori_loop(0, NC, pack_wells, 0)

    def part2(buf, s):
        return buf.at[s, pl.ds(0, RPAIR // 2)]

    def wait_wells(sem, n):
        both = rbuf2.at[pl.ds(0, n), pl.ds(0, RPAIR // 2)]
        pltpu.make_async_copy(both, both, sem).wait()

    own2 = pltpu.make_async_copy(part2(sbuf2, me), part2(rbuf2, 0), lsem2)
    own2.start()
    waiting = [n for n in ORDER if n]

    def send_wells(count):
        for n in waiting[:count]:
            dz = steps_z(n // GB) * (1 - 2 * (n % 2))
            to = col(my + n % GB // 2, mz + NZ + dz, mc + n)
            copy_to(part2(sbuf2, to), part2(rbuf2, n), ssem2, rsem2.at[n // GB], to).start()
        del waiting[:count]

    send_wells(EARLY)

    def split_u(c, carry):
        at = pl.ds(pl.multiple_of(512 * c, 512), 512)
        hi, lo = split(u[:, at])
        u2[0, :, at] = hi
        u2[1, :, at] = lo
        return carry

    lax.fori_loop(0, NC * 2 * K // 512, split_u, 0)

    def basis_block(g, carry):
        at = pl.ds(pl.multiple_of(GB * K * g, S), GB * K)
        tiles = [v[slot_s[source_s[GB * g + j]]] for j in range(GB)]
        for half in range(2):
            x = jnp.concatenate([t[K * half : K * half + K] for t in tiles], 0).T
            hi, lo = split(x)
            vt[0, half, :, at] = hi
            vt[1, half, :, at] = lo
        return carry

    lax.fori_loop(0, NGB, basis_block, 0)

    field_o[...] = jnp.zeros_like(field_o)

    def field_group(g):
        parts = []
        for i in range(GS):
            s = GS * g + i
            rr = rrr[s]
            x = rbuf[s]
            parts.append(jnp.where(rows48f < rr[0:1], x[:K], 0.0))
            parts.append(jnp.where(rows48f < rr[1:2], flipped(x[MID:]), 0.0))
        hi, lo = split(jnp.concatenate(parts, 0))
        at = pl.ds(pl.multiple_of(GS * 2 * K * g, S), GS * 2 * K)
        p = dot(u2[0, :, at], jnp.concatenate([hi, lo], 1))
        q = dot(u2[1, :, at], hi)
        field_o[...] += p[:, :S] + p[:, S:] + q

    def field_loop(k, c):
        g = (mg - k + NG) % NG
        wait_for(rbuf, rsem.at[g], GS)
        field_group(g)
        return c

    lax.fori_loop(1, NG, field_loop, 0)
    own.wait()
    wait_for(rbuf, rsem.at[mg], GS - 1)
    field_group(mg)

    def at_well(w, c):
        gacc[pl.ds(w, 1), :] = field_o[pl.ds(wells_s[w], 1), :]
        return c

    lax.fori_loop(0, WPT, at_well, 0)
    e = jnp.exp(gacc[:WPT])
    wag[me] = (e - obs[...]) * e / 0.25
    gacc[...] = jnp.zeros_like(gacc)

    def gradient_group(g):
        pa, pb = [], []
        for j in range(GB):
            c = col(my + NY - j // 2, mz + NZ - steps_z(g), mc + j)
            q = slot_s[c]
            m = rbuf2[GB * g + j]
            hi = m.astype(BF16).astype(F32)
            lo = m - hi
            turned = pltpu.roll(lo, WPT, 1)
            one = jnp.where(left, hi[:TOP], turned[:TOP])
            end = jnp.where(left8, hi[TOP:], turned[TOP:])
            turned = pltpu.roll(hi, WPT, 1)
            two = jnp.where(left, turned[:TOP], lo[:TOP])
            end2 = jnp.where(left8, turned[TOP:], lo[TOP:])
            end = jnp.where(upper8, end, pltpu.roll(end2, 4, 0))
            rows = jnp.concatenate([one, two, end], 0).astype(BF16)
            whi, wlo = split(wag[c])
            w2 = jnp.concatenate(
                [
                    jnp.concatenate([whi, wlo], 1),
                    jnp.concatenate([whi, jnp.zeros_like(whi)], 1),
                ],
                0,
            )
            p = dot(rows, w2)
            adj = p[:, :S] + p[:, S:]
            pa.append(jnp.where(rows48 < ranks_s[0, q], adj[:K], 0.0))
            pb.append(jnp.where(rows48 < ranks_s[1, q], flipped(adj[MID:RPAIR]), 0.0))
        at = pl.ds(GB * K * g, GB * K)
        for half, parts in ((0, pa), (1, pb)):
            hi, lo = split(jnp.concatenate(parts, 0))
            p = dot(vt[0, half, :, at], jnp.concatenate([hi, lo], 1))
            q = dot(vt[1, half, :, at], hi)
            gacc[B * half : B * half + B, :] += p[:, :S] + p[:, S:] + q

    partner = col(my, mz, mc + 1)

    def pass_on(s, rs, to):
        copy_to(wag.at[s], wag.at[s], agsem, rs, to).start()

    def source(dy, i):
        return col(my + NY - dy, mz + NZ - steps_z(i), mc)

    def own_piece(i):
        for dy in (1, 3):
            pass_on(source(0, i), yrsem.at[dy * NZ + i], col(my + dy, mz, mc))
        pass_on(source(0, i), prsem.at[OTHER[i]], partner)

    def along(way):
        return col(my, mz + NZ + way, mc)

    for i in range(1, 5):
        pass_on(me, zrsem.at[i], along(steps_z(i)))
    own_piece(0)
    for step in range(NZ + LAG):
        i = step
        if 1 <= i < NZ:
            wait_for(wag, zrsem.at[i], 1)
            if i == 3:
                pass_on(source(0, i), zrsem.at[5], along(ahead))
                pass_on(source(0, i), zrsem.at[7], along(2 * ahead))
            if i == 4:
                pass_on(source(0, i), zrsem.at[6], along(-ahead))
            own_piece(i)
        i = step - 2
        if 0 <= i < NZ:
            for dy in (1, 3):
                wait_for(wag, yrsem.at[dy * NZ + i], 1)
                if dy == (3 if i % 2 else 1):
                    pass_on(source(dy, i), yrsem.at[2 * NZ + i], col(my + dy, mz, mc))
                pass_on(source(dy, i), prsem.at[OTHER[i]], partner)
        i = step - 4
        if 0 <= i < NZ:
            wait_for(wag, yrsem.at[2 * NZ + i], 1)
            pass_on(source(2, i), prsem.at[OTHER[i]], partner)
        send_wells(PACE)
        i = step - LAG
        if 0 <= i < NZ:
            wait_for(wag, prsem.at[i], NY)
            if i == 0:
                own2.wait()
            wait_wells(rsem2.at[i], GB if i else GB - 1)
            gradient_group(i)

    part = 2 * B // NR

    def exchange(d):
        to = (row + d) % NR
        return pltpu.make_async_remote_copy(
            src_ref=gacc.at[pl.ds(pl.multiple_of(part * to, part), part)],
            dst_ref=xrecv.at[d - 1],
            send_sem=xssem.at[d - 1],
            recv_sem=xrsem.at[d - 1],
            device_id=(me, to),
            device_id_type=MESH,
        )

    moves = [exchange(d) for d in range(1, NR)]
    for m in moves:
        m.start()
    mine = pl.ds(pl.multiple_of(part * row, part), part)
    total = lat[mine, :] + gacc[mine, :]
    for d in range(1, NR):
        moves[d - 1].wait_recv()
        total += xrecv[d - 1]
    grad_o[...] = total
    for m in moves:
        m.wait_send()
    wait_for(sbuf, ssem, NC - 1)
    wait_wells(ssem2, NC - 1)
    wait_for(rrs, rrssem, NC - 1)
    wait_for(wag, agsem, NC - 1)


def hand_over(field, gradient, field_o, grad_o):
    field_o[...] = field[...]
    grad_o[...] = gradient[...]


def on_device(latent, v_basis, u_basis, ranks, slot_row, wells, observed):
    vmem = pl.BlockSpec(memory_space=pltpu.VMEM)
    smem = pl.BlockSpec(memory_space=pltpu.SMEM)
    anywhere = pl.BlockSpec(memory_space=pl.ANY)
    dma = pltpu.SemaphoreType.DMA
    field, gradient = pl.pallas_call(
        kernel,
        name="tlr",
        out_shape=(
            jax.ShapeDtypeStruct((B, S), F32),
            jax.ShapeDtypeStruct((2 * B // NR, S), F32),
        ),
        in_specs=[smem, smem, smem, vmem, vmem, anywhere, anywhere],
        out_specs=(vmem, vmem),
        scratch_shapes=[
            pltpu.VMEM((NC, 2 * K, B), F32),
            pltpu.VMEM((B, NC * 2 * K), F32),
            pltpu.VMEM((2 * B, 2 * S), BF16),
            pltpu.VMEM((2, B, NC * 2 * K), BF16),
            pltpu.VMEM((2 * WPT, NC * 2 * K), F32),
            pltpu.VMEM((NC * 2 * K, S), F32),
            pltpu.VMEM((2, 2, B, NC * K), BF16),
            pltpu.VMEM((NC, RPAIR, S), F32),
            pltpu.VMEM((NC, RPAIR, S), F32),
            pltpu.VMEM((NC, HALF, S), F32),
            pltpu.VMEM((NC, HALF, S), F32),
            pltpu.VMEM((NC, 2, S), F32),
            pltpu.VMEM((NC, 2, S), F32),
            pltpu.VMEM((NC, WPT, S), F32),
            pltpu.VMEM((2 * B, S), F32),
            pltpu.VMEM((NR - 1, 2 * B // NR, S), F32),
            dma, dma, dma, dma, dma, dma((NG,)), dma, dma, dma, dma((NGB,)),
            dma, dma((NZ,)), dma((NY * NZ,)), dma((NZ,)), pltpu.SMEM((NC,), jnp.int32),
            dma((NR - 1,)), dma((NR - 1,)),
        ],
        compiler_params=pltpu.CompilerParams(
            collective_id=0, has_side_effects=True, vmem_limit_bytes=60 * 2**20
        ),
    )(
        slot_row[0],
        ranks[:, 0].T,
        wells[0, 0],
        latent,
        observed[0, 0],
        v_basis.reshape(NC, 2 * K, B),
        u_basis[0, 0],
    )
    field, gradient = pl.pallas_call(
        hand_over,
        name="hand_over",
        out_shape=(
            jax.ShapeDtypeStruct(field.shape, F32),
            jax.ShapeDtypeStruct(gradient.shape, F32),
        ),
        in_specs=[vmem, vmem],
        out_specs=(vmem, vmem),
    )(field, gradient)
    return (field[None, None], gradient)


def solution(mesh):
    placed = (
        P("col", None),
        P(None, "row", "col", None, None),
        P("col", "row", None, None),
        P(None, "row", "col"),
        P("row", None),
        P("col", "row", None),
        P("col", "row", None, None),
    )
    return jax.shard_map(
        on_device,
        mesh=mesh,
        in_specs=placed,
        out_specs=(P("col", "row", None, None), P(("col", "row"), None)),
        check_vma=False,
    )
```

```python
import jax
import jax.numpy as jnp
from jax import lax
from jax.experimental import pallas as pl
from jax.experimental.pallas import tpu as pltpu
from jax.sharding import PartitionSpec as P

MESH = pl.DeviceIdType.MESH
F32, BF16 = jnp.float32, jnp.bfloat16
K = 48
RPAIR = 72
MID = RPAIR - K
S = 128
B = 256
NC = 64
NR = 4
GS = 4
NG = NC // GS
GB = 8
NGB = NC // GB
NY = 4
NZ = 8
WPT = 64
HALF = 40
TOP = 32
EARLY = 12
PACE = 8
LAG = 6
ORDER = [GB * g + n for g in (7, 6, 0, 1, 2, 3, 4, 5) for n in range(GB)]
OTHER = (0, 2, 1, 4, 3, 6, 5, 7)


def split(x):
    hi = x.astype(BF16)
    return hi, (x - hi.astype(F32)).astype(BF16)


def dot(a, b):
    return jnp.dot(a, b, preferred_element_type=F32)


def flipped(x):
    v = x.reshape(K // 8, 8, S)
    i = lax.broadcasted_iota(jnp.int32, (K // 8, 8, S), 1)
    for step in (1, 2, 4):
        v = jnp.where((i & step) == 0, pltpu.roll(v, 8 - step, 1), pltpu.roll(v, step, 1))
    return jnp.concatenate([v[K // 8 - 1 - t] for t in range(K // 8)], 0)


def pack(a, b):
    r = flipped(b)
    return jnp.concatenate([a[:MID], a[MID:] + r[:MID], r[MID:]], 0)


def kernel(
    slot_s, ranks_s, wells_s, lat_hbm, obs_hbm, v_hbm, u_hbm, field_o, grad_o,
    v, u, l2, u2, ur, ut, vt, sbuf, rbuf, sbuf2, rbuf2, rrs, rrr, wag, gacc, xrecv,
    lat, obs, latsem, obssem, vsem, usem, lsem, lsem2, ssem, rsem, rrssem, rrrsem, ssem2, rsem2, agsem, zrsem, yrsem, prsem, source_s, xssem, xrsem,
):
    me = lax.axis_index("col")
    row = lax.axis_index("row")
    mg = me // GS
    mu = me % GS
    my = me // (NZ * 2)
    mz = me // 2 % NZ
    mc = me % 2
    latcopy = pltpu.make_async_copy(lat_hbm, lat, latsem)
    latcopy.start()
    vcopy = pltpu.make_async_copy(v_hbm, v, vsem)
    vcopy.start()
    ucopy = pltpu.make_async_copy(u_hbm, u, usem)

    barrier = pltpu.get_barrier_semaphore()

    def greet(i, c):
        pl.semaphore_signal(barrier, inc=1, device_id=((me + i) % NC, row), device_id_type=MESH)
        return c

    lax.fori_loop(1, NC, greet, 0)
    for i in range(1, NR):
        pl.semaphore_signal(barrier, inc=1, device_id=(me, (row + i) % NR), device_id_type=MESH)

    rows48 = lax.broadcasted_iota(jnp.int32, (K, S), 0)
    rows48f = rows48.astype(F32)

    latcopy.wait()
    lhi, llo = split(lat[...])
    l2[:, :S] = lhi
    l2[:, S:] = llo

    def peer(k, i):
        return GS * ((mg + k) % NG) + (i + mu) % GS

    def copy_to(src, dst, ss, rs, col):
        return pltpu.make_async_remote_copy(
            src_ref=src,
            dst_ref=dst,
            send_sem=ss,
            recv_sem=rs,
            device_id=(col, row),
            device_id_type=MESH,
        )

    def wait_for(buf, sem, n):
        pltpu.make_async_copy(buf.at[pl.ds(0, n)], buf.at[pl.ds(0, n)], sem).wait()

    def rank_row(k, c):
        for i in range(GS):
            q = slot_s[peer(k, i)]
            first = lax.broadcasted_iota(jnp.int32, (2, S), 0) == 0
            rrs[GS * k + i] = jnp.where(first, ranks_s[0, q], ranks_s[1, q]).astype(F32)
        return c

    lax.fori_loop(0, NG, rank_row, 0)
    rrr[me] = rrs[0]

    def col(y, z, c):
        return y % NY * (NZ * 2) + z % NZ * 2 + c % 2

    ahead = 1 - 2 * mc

    def steps_z(i):
        return (ahead if i % 2 else -ahead) * ((i + 1) // 2)

    for i in range(NGB):
        for n in range(GB):
            source_s[GB * i + n] = col(my + NY - n // 2, mz + NZ - steps_z(i), mc + n)

    vcopy.wait()
    ucopy.start()
    obscopy = pltpu.make_async_copy(obs_hbm, obs, obssem)
    obscopy.start()

    def products(x, half):
        hi, lo = split(x)
        n = x.shape[0]
        p = dot(jnp.concatenate([hi, lo], 0), l2[B * half : B * half + B, :])
        return p[:n, :S] + p[:n, S:] + p[n:, :S]

    def forward(k):
        qs = [slot_s[peer(k, i)] for i in range(GS)]
        tiles = [v[q] for q in qs]
        a = products(jnp.concatenate([x[:K] for x in tiles], 0), 0)
        b = products(jnp.concatenate([x[K:] for x in tiles], 0), 1)
        for i in range(GS):
            ai = jnp.where(rows48 < ranks_s[0, qs[i]], a[K * i : K * i + K], 0.0)
            bi = jnp.where(rows48 < ranks_s[1, qs[i]], b[K * i : K * i + K], 0.0)
            sbuf[GS * k + i] = pack(ai, bi)

    def send(k, i):
        copy_to(sbuf.at[GS * k + i], rbuf.at[me], ssem, rsem.at[mg], peer(k, i)).start()

    def send_ranks(k, i):
        copy_to(rrs.at[GS * k + i], rrr.at[me], rrssem, rrrsem, peer(k, i)).start()

    forward(0)
    pl.semaphore_wait(barrier, NC - 1 + NR - 1)
    for i in range(1, GS):
        send_ranks(0, i)

    def ranks_loop(k, c):
        for i in range(GS):
            send_ranks(k, i)
        return c

    lax.fori_loop(1, NG, ranks_loop, 0)

    forward(1)
    own = pltpu.make_async_copy(sbuf.at[0], rbuf.at[me], lsem)
    own.start()
    for i in range(1, GS):
        send(0, i)

    def forward_loop(k, c):
        forward(k)
        for i in range(GS):
            send(k - 1, i)
        return c

    lax.fori_loop(2, NG, forward_loop, 0)
    for i in range(GS):
        send(NG - 1, i)

    ucopy.wait()

    def well_row(w, c):
        at = u[pl.ds(wells_s[w], 1), :]
        ur[pl.ds(w, 1), :] = at
        ur[pl.ds(w + WPT, 1), :] = at
        return c

    lax.fori_loop(0, WPT, well_row, 0)

    def well_block(c, carry):
        at = pl.ds(pl.multiple_of(S * c, S), S)
        ut[at, :] = ur[:, at].T
        return carry

    lax.fori_loop(0, NC * 2 * K // S, well_block, 0)
    wait_for(rrr, rrrsem, NC - 1)
    left = lax.broadcasted_iota(jnp.int32, (TOP, S), 1) < WPT
    left8 = lax.broadcasted_iota(jnp.int32, (8, S), 1) < WPT
    upper8 = lax.broadcasted_iota(jnp.int32, (8, S), 0) < 4

    def pack_wells(j, carry):
        rr = rrr[j]
        x = ut[pl.ds(pl.multiple_of(2 * K * j, 2 * K), 2 * K), :]
        p = pack(
            jnp.where(rows48f < rr[0:1], x[:K], 0.0),
            jnp.where(rows48f < rr[1:2], x[K:], 0.0),
        )
        sbuf2[j, :TOP] = jnp.where(left, p[:TOP], p[TOP : 2 * TOP])
        end = p[2 * TOP :]
        sbuf2[j, TOP:] = jnp.where(left8, end, pltpu.roll(end, 4, 0))
        return carry

    lax.fori_loop(0, NC, pack_wells, 0)

    def part2(buf, s):
        return buf.at[s, pl.ds(0, RPAIR // 2)]

    def wait_wells(sem, n):
        both = rbuf2.at[pl.ds(0, n), pl.ds(0, RPAIR // 2)]
        pltpu.make_async_copy(both, both, sem).wait()

    own2 = pltpu.make_async_copy(part2(sbuf2, me), part2(rbuf2, 0), lsem2)
    own2.start()
    waiting = [n for n in ORDER if n]

    def send_wells(count):
        for n in waiting[:count]:
            dz = steps_z(n // GB) * (1 - 2 * (n % 2))
            to = col(my + n % GB // 2, mz + NZ + dz, mc + n)
            copy_to(part2(sbuf2, to), part2(rbuf2, n), ssem2, rsem2.at[n // GB], to).start()
        del waiting[:count]

    send_wells(EARLY)

    def split_u(c, carry):
        at = pl.ds(pl.multiple_of(512 * c, 512), 512)
        hi, lo = split(u[:, at])
        u2[0, :, at] = hi
        u2[1, :, at] = lo
        return carry

    lax.fori_loop(0, NC * 2 * K // 512, split_u, 0)

    def basis_block(g, carry):
        at = pl.ds(pl.multiple_of(GB * K * g, S), GB * K)
        tiles = [v[slot_s[source_s[GB * g + j]]] for j in range(GB)]
        for half in range(2):
            x = jnp.concatenate([t[K * half : K * half + K] for t in tiles], 0).T
            hi, lo = split(x)
            vt[0, half, :, at] = hi
            vt[1, half, :, at] = lo
        return carry

    lax.fori_loop(0, NGB, basis_block, 0)

    field_o[...] = jnp.zeros_like(field_o)

    def field_group(g):
        parts = []
        for i in range(GS):
            s = GS * g + i
            rr = rrr[s]
            x = rbuf[s]
            parts.append(jnp.where(rows48f < rr[0:1], x[:K], 0.0))
            parts.append(jnp.where(rows48f < rr[1:2], flipped(x[MID:]), 0.0))
        hi, lo = split(jnp.concatenate(parts, 0))
        at = pl.ds(pl.multiple_of(GS * 2 * K * g, S), GS * 2 * K)
        p = dot(u2[0, :, at], jnp.concatenate([hi, lo], 1))
        q = dot(u2[1, :, at], hi)
        field_o[...] += p[:, :S] + p[:, S:] + q

    def field_loop(k, c):
        g = (mg - k + NG) % NG
        wait_for(rbuf, rsem.at[g], GS)
        field_group(g)
        return c

    lax.fori_loop(1, NG, field_loop, 0)
    own.wait()
    wait_for(rbuf, rsem.at[mg], GS - 1)
    field_group(mg)

    def at_well(w, c):
        gacc[pl.ds(w, 1), :] = field_o[pl.ds(wells_s[w], 1), :]
        return c

    lax.fori_loop(0, WPT, at_well, 0)
    obscopy.wait()
    e = jnp.exp(gacc[:WPT])
    wag[me] = (e - obs[...]) * e / 0.25
    gacc[...] = jnp.zeros_like(gacc)

    def gradient_group(g):
        pa, pb = [], []
        for j in range(GB):
            c = col(my + NY - j // 2, mz + NZ - steps_z(g), mc + j)
            q = slot_s[c]
            m = rbuf2[GB * g + j]
            hi = m.astype(BF16).astype(F32)
            lo = m - hi
            turned = pltpu.roll(lo, WPT, 1)
            one = jnp.where(left, hi[:TOP], turned[:TOP])
            end = jnp.where(left8, hi[TOP:], turned[TOP:])
            turned = pltpu.roll(hi, WPT, 1)
            two = jnp.where(left, turned[:TOP], lo[:TOP])
            end2 = jnp.where(left8, turned[TOP:], lo[TOP:])
            end = jnp.where(upper8, end, pltpu.roll(end2, 4, 0))
            rows = jnp.concatenate([one, two, end], 0).astype(BF16)
            whi, wlo = split(wag[c])
            w2 = jnp.concatenate(
                [
                    jnp.concatenate([whi, wlo], 1),
                    jnp.concatenate([whi, jnp.zeros_like(whi)], 1),
                ],
                0,
            )
            p = dot(rows, w2)
            adj = p[:, :S] + p[:, S:]
            pa.append(jnp.where(rows48 < ranks_s[0, q], adj[:K], 0.0))
            pb.append(jnp.where(rows48 < ranks_s[1, q], flipped(adj[MID:RPAIR]), 0.0))
        at = pl.ds(GB * K * g, GB * K)
        for half, parts in ((0, pa), (1, pb)):
            hi, lo = split(jnp.concatenate(parts, 0))
            p = dot(vt[0, half, :, at], jnp.concatenate([hi, lo], 1))
            q = dot(vt[1, half, :, at], hi)
            gacc[B * half : B * half + B, :] += p[:, :S] + p[:, S:] + q

    partner = col(my, mz, mc + 1)

    def pass_on(s, rs, to):
        copy_to(wag.at[s], wag.at[s], agsem, rs, to).start()

    def source(dy, i):
        return col(my + NY - dy, mz + NZ - steps_z(i), mc)

    def own_piece(i):
        for dy in (1, 3):
            pass_on(source(0, i), yrsem.at[dy * NZ + i], col(my + dy, mz, mc))
        pass_on(source(0, i), prsem.at[OTHER[i]], partner)

    def along(way):
        return col(my, mz + NZ + way, mc)

    for i in range(1, 5):
        pass_on(me, zrsem.at[i], along(steps_z(i)))
    own_piece(0)
    for step in range(NZ + LAG):
        i = step
        if 1 <= i < NZ:
            wait_for(wag, zrsem.at[i], 1)
            if i == 3:
                pass_on(source(0, i), zrsem.at[5], along(ahead))
                pass_on(source(0, i), zrsem.at[7], along(2 * ahead))
            if i == 4:
                pass_on(source(0, i), zrsem.at[6], along(-ahead))
            own_piece(i)
        i = step - 2
        if 0 <= i < NZ:
            for dy in (1, 3):
                wait_for(wag, yrsem.at[dy * NZ + i], 1)
                if dy == (3 if i % 2 else 1):
                    pass_on(source(dy, i), yrsem.at[2 * NZ + i], col(my + dy, mz, mc))
                pass_on(source(dy, i), prsem.at[OTHER[i]], partner)
        i = step - 4
        if 0 <= i < NZ:
            wait_for(wag, yrsem.at[2 * NZ + i], 1)
            pass_on(source(2, i), prsem.at[OTHER[i]], partner)
        send_wells(PACE)
        i = step - LAG
        if 0 <= i < NZ:
            wait_for(wag, prsem.at[i], NY)
            if i == 0:
                own2.wait()
            wait_wells(rsem2.at[i], GB if i else GB - 1)
            gradient_group(i)

    part = 2 * B // NR

    def exchange(d):
        to = (row + d) % NR
        return pltpu.make_async_remote_copy(
            src_ref=gacc.at[pl.ds(pl.multiple_of(part * to, part), part)],
            dst_ref=xrecv.at[d - 1],
            send_sem=xssem.at[d - 1],
            recv_sem=xrsem.at[d - 1],
            device_id=(me, to),
            device_id_type=MESH,
        )

    moves = [exchange(d) for d in range(1, NR)]
    for m in moves:
        m.start()
    mine = pl.ds(pl.multiple_of(part * row, part), part)
    total = lat[mine, :] + gacc[mine, :]
    for d in range(1, NR):
        moves[d - 1].wait_recv()
        total += xrecv[d - 1]
    grad_o[...] = total
    for m in moves:
        m.wait_send()
    wait_for(sbuf, ssem, NC - 1)
    wait_wells(ssem2, NC - 1)
    wait_for(rrs, rrssem, NC - 1)
    wait_for(wag, agsem, NC - 1)


def hand_over(field, gradient, field_o, grad_o):
    field_o[...] = field[...]
    grad_o[...] = gradient[...]


def on_device(latent, v_basis, u_basis, ranks, slot_row, wells, observed):
    vmem = pl.BlockSpec(memory_space=pltpu.VMEM)
    smem = pl.BlockSpec(memory_space=pltpu.SMEM)
    anywhere = pl.BlockSpec(memory_space=pl.ANY)
    dma = pltpu.SemaphoreType.DMA
    field, gradient = pl.pallas_call(
        kernel,
        name="tlr",
        out_shape=(
            pltpu.VMEM((B, S), F32),
            pltpu.VMEM((2 * B // NR, S), F32),
        ),
        in_specs=[smem, smem, smem, anywhere, anywhere, anywhere, anywhere],
        out_specs=(vmem, vmem),
        scratch_shapes=[
            pltpu.VMEM((NC, 2 * K, B), F32),
            pltpu.VMEM((B, NC * 2 * K), F32),
            pltpu.VMEM((2 * B, 2 * S), BF16),
            pltpu.VMEM((2, B, NC * 2 * K), BF16),
            pltpu.VMEM((2 * WPT, NC * 2 * K), F32),
            pltpu.VMEM((NC * 2 * K, S), F32),
            pltpu.VMEM((2, 2, B, NC * K), BF16),
            pltpu.VMEM((NC, RPAIR, S), F32),
            pltpu.VMEM((NC, RPAIR, S), F32),
            pltpu.VMEM((NC, HALF, S), F32),
            pltpu.VMEM((NC, HALF, S), F32),
            pltpu.VMEM((NC, 2, S), F32),
            pltpu.VMEM((NC, 2, S), F32),
            pltpu.VMEM((NC, WPT, S), F32),
            pltpu.VMEM((2 * B, S), F32),
            pltpu.VMEM((NR - 1, 2 * B // NR, S), F32),
            pltpu.VMEM((2 * B, S), F32),
            pltpu.VMEM((WPT, S), F32),
            dma, dma, dma, dma, dma, dma, dma, dma((NG,)), dma, dma, dma, dma((NGB,)),
            dma, dma((NZ,)), dma((NY * NZ,)), dma((NZ,)), pltpu.SMEM((NC,), jnp.int32),
            dma((NR - 1,)), dma((NR - 1,)),
        ],
        compiler_params=pltpu.CompilerParams(
            collective_id=0, has_side_effects=True, vmem_limit_bytes=60 * 2**20
        ),
    )(
        slot_row[0],
        ranks[:, 0].T,
        wells[0, 0],
        latent,
        observed[0, 0],
        v_basis.reshape(NC, 2 * K, B),
        u_basis[0, 0],
    )
    field, gradient = pl.pallas_call(
        hand_over,
        name="hand_over",
        out_shape=(
            jax.ShapeDtypeStruct(field.shape, F32),
            jax.ShapeDtypeStruct(gradient.shape, F32),
        ),
        in_specs=[vmem, vmem],
        out_specs=(vmem, vmem),
    )(
        pltpu.with_memory_space_constraint(field, pltpu.VMEM),
        pltpu.with_memory_space_constraint(gradient, pltpu.VMEM),
    )
    return (field[None, None], gradient)


def solution(mesh):
    placed = (
        P("col", None),
        P(None, "row", "col", None, None),
        P("col", "row", None, None),
        P(None, "row", "col"),
        P("row", None),
        P("col", "row", None),
        P("col", "row", None, None),
    )
    return jax.shard_map(
        on_device,
        mesh=mesh,
        in_specs=placed,
        out_specs=(P("col", "row", None, None), P(("col", "row"), None)),
        check_vma=False,
    )
```

```python
import jax
import jax.numpy as jnp
from jax import lax
from jax.experimental import pallas as pl
from jax.experimental.pallas import tpu as pltpu
from jax.sharding import PartitionSpec as P

MESH = pl.DeviceIdType.MESH
F32, BF16 = jnp.float32, jnp.bfloat16
K = 48
RPAIR = 72
MID = RPAIR - K
S = 128
B = 256
NC = 64
NR = 4
GS = 4
NG = NC // GS
GB = 8
NGB = NC // GB
NY = 4
NZ = 8
WPT = 64
HALF = 40
TOP = 32
EARLY = 12
PACE = 8
LAG = 6
ORDER = [GB * g + n for g in (0, 7, 6, 1, 2, 3, 4, 5) for n in range(GB)]
OTHER = (0, 2, 1, 4, 3, 6, 5, 7)


def split(x):
    hi = x.astype(BF16)
    return hi, (x - hi.astype(F32)).astype(BF16)


def dot(a, b):
    return jnp.dot(a, b, preferred_element_type=F32)


def flipped(x):
    v = x.reshape(K // 8, 8, S)
    i = lax.broadcasted_iota(jnp.int32, (K // 8, 8, S), 1)
    for step in (1, 2, 4):
        v = jnp.where((i & step) == 0, pltpu.roll(v, 8 - step, 1), pltpu.roll(v, step, 1))
    return jnp.concatenate([v[K // 8 - 1 - t] for t in range(K // 8)], 0)


def pack(a, b):
    r = flipped(b)
    return jnp.concatenate([a[:MID], a[MID:] + r[:MID], r[MID:]], 0)


def kernel(
    slot_s, ranks_s, wells_s, lat_hbm, obs_hbm, v_hbm, u_hbm, field_o, grad_o,
    v, u, l2, u2, ur, ut, vt, sbuf, rbuf, sbuf2, rbuf2, rrs, rrr, wag, gacc, xrecv,
    lat, obs, latsem, obssem, vsem, usem, lsem, lsem2, ssem, rsem, rrssem, rrrsem, ssem2, rsem2, agsem, zrsem, yrsem, prsem, source_s, xssem, xrsem,
):
    me = lax.axis_index("col")
    row = lax.axis_index("row")
    mg = me // GS
    mu = me % GS
    my = me // (NZ * 2)
    mz = me // 2 % NZ
    mc = me % 2
    latcopy = pltpu.make_async_copy(lat_hbm, lat, latsem)
    latcopy.start()
    vcopy = pltpu.make_async_copy(v_hbm, v, vsem)
    vcopy.start()
    ucopy = pltpu.make_async_copy(u_hbm, u, usem)

    barrier = pltpu.get_barrier_semaphore()

    def greet(i, c):
        pl.semaphore_signal(barrier, inc=1, device_id=((me + i) % NC, row), device_id_type=MESH)
        return c

    lax.fori_loop(1, NC, greet, 0)
    for i in range(1, NR):
        pl.semaphore_signal(barrier, inc=1, device_id=(me, (row + i) % NR), device_id_type=MESH)

    rows48 = lax.broadcasted_iota(jnp.int32, (K, S), 0)
    rows48f = rows48.astype(F32)

    latcopy.wait()
    lhi, llo = split(lat[...])
    l2[:, :S] = lhi
    l2[:, S:] = llo

    def peer(k, i):
        return GS * ((mg + k) % NG) + (i + mu) % GS

    def copy_to(src, dst, ss, rs, col):
        return pltpu.make_async_remote_copy(
            src_ref=src,
            dst_ref=dst,
            send_sem=ss,
            recv_sem=rs,
            device_id=(col, row),
            device_id_type=MESH,
        )

    def wait_for(buf, sem, n):
        pltpu.make_async_copy(buf.at[pl.ds(0, n)], buf.at[pl.ds(0, n)], sem).wait()

    def rank_row(k, c):
        for i in range(GS):
            q = slot_s[peer(k, i)]
            first = lax.broadcasted_iota(jnp.int32, (2, S), 0) == 0
            rrs[GS * k + i] = jnp.where(first, ranks_s[0, q], ranks_s[1, q]).astype(F32)
        return c

    lax.fori_loop(0, NG, rank_row, 0)
    rrr[me] = rrs[0]

    def col(y, z, c):
        return y % NY * (NZ * 2) + z % NZ * 2 + c % 2

    ahead = 1 - 2 * mc

    def steps_z(i):
        return (ahead if i % 2 else -ahead) * ((i + 1) // 2)

    for i in range(NGB):
        for n in range(GB):
            source_s[GB * i + n] = col(my + NY - n // 2, mz + NZ - steps_z(i), mc + n)

    vcopy.wait()
    ucopy.start()
    obscopy = pltpu.make_async_copy(obs_hbm, obs, obssem)
    obscopy.start()

    def products(x, half):
        hi, lo = split(x)
        n = x.shape[0]
        p = dot(jnp.concatenate([hi, lo], 0), l2[B * half : B * half + B, :])
        return p[:n, :S] + p[:n, S:] + p[n:, :S]

    def forward(k):
        qs = [slot_s[peer(k, i)] for i in range(GS)]
        tiles = [v[q] for q in qs]
        a = products(jnp.concatenate([x[:K] for x in tiles], 0), 0)
        b = products(jnp.concatenate([x[K:] for x in tiles], 0), 1)
        for i in range(GS):
            ai = jnp.where(rows48 < ranks_s[0, qs[i]], a[K * i : K * i + K], 0.0)
            bi = jnp.where(rows48 < ranks_s[1, qs[i]], b[K * i : K * i + K], 0.0)
            sbuf[GS * k + i] = pack(ai, bi)

    def send(k, i):
        copy_to(sbuf.at[GS * k + i], rbuf.at[me], ssem, rsem.at[mg], peer(k, i)).start()

    def send_ranks(k, i):
        copy_to(rrs.at[GS * k + i], rrr.at[me], rrssem, rrrsem, peer(k, i)).start()

    forward(0)
    pl.semaphore_wait(barrier, NC - 1 + NR - 1)
    for i in range(1, GS):
        send_ranks(0, i)

    def ranks_loop(k, c):
        for i in range(GS):
            send_ranks(k, i)
        return c

    lax.fori_loop(1, NG, ranks_loop, 0)

    forward(1)
    own = pltpu.make_async_copy(sbuf.at[0], rbuf.at[me], lsem)
    own.start()
    for i in range(1, GS):
        send(0, i)

    def forward_loop(k, c):
        forward(k)
        for i in range(GS):
            send(k - 1, i)
        return c

    lax.fori_loop(2, NG, forward_loop, 0)
    for i in range(GS):
        send(NG - 1, i)

    ucopy.wait()

    def well_row(w, c):
        at = u[pl.ds(wells_s[w], 1), :]
        ur[pl.ds(w, 1), :] = at
        ur[pl.ds(w + WPT, 1), :] = at
        return c

    lax.fori_loop(0, WPT, well_row, 0)

    def well_block(c, carry):
        at = pl.ds(pl.multiple_of(S * c, S), S)
        ut[at, :] = ur[:, at].T
        return carry

    lax.fori_loop(0, NC * 2 * K // S, well_block, 0)
    wait_for(rrr, rrrsem, NC - 1)
    left = lax.broadcasted_iota(jnp.int32, (TOP, S), 1) < WPT
    left8 = lax.broadcasted_iota(jnp.int32, (8, S), 1) < WPT
    upper8 = lax.broadcasted_iota(jnp.int32, (8, S), 0) < 4

    def pack_wells(j, carry):
        rr = rrr[j]
        x = ut[pl.ds(pl.multiple_of(2 * K * j, 2 * K), 2 * K), :]
        p = pack(
            jnp.where(rows48f < rr[0:1], x[:K], 0.0),
            jnp.where(rows48f < rr[1:2], x[K:], 0.0),
        )
        sbuf2[j, :TOP] = jnp.where(left, p[:TOP], p[TOP : 2 * TOP])
        end = p[2 * TOP :]
        sbuf2[j, TOP:] = jnp.where(left8, end, pltpu.roll(end, 4, 0))
        return carry

    lax.fori_loop(0, NC, pack_wells, 0)

    def part2(buf, s):
        return buf.at[s, pl.ds(0, RPAIR // 2)]

    def wait_wells(sem, n):
        both = rbuf2.at[pl.ds(0, n), pl.ds(0, RPAIR // 2)]
        pltpu.make_async_copy(both, both, sem).wait()

    own2 = pltpu.make_async_copy(part2(sbuf2, me), part2(rbuf2, 0), lsem2)
    own2.start()
    waiting = [n for n in ORDER if n]

    def send_wells(count):
        for n in waiting[:count]:
            dz = steps_z(n // GB) * (1 - 2 * (n % 2))
            to = col(my + n % GB // 2, mz + NZ + dz, mc + n)
            copy_to(part2(sbuf2, to), part2(rbuf2, n), ssem2, rsem2.at[n // GB], to).start()
        del waiting[:count]

    send_wells(EARLY)

    def split_u(c, carry):
        at = pl.ds(pl.multiple_of(512 * c, 512), 512)
        hi, lo = split(u[:, at])
        u2[0, :, at] = hi
        u2[1, :, at] = lo
        return carry

    lax.fori_loop(0, NC * 2 * K // 512, split_u, 0)

    def basis_block(g, carry):
        wide = GB * K
        tiles = [v[slot_s[source_s[GB * g + j]]] for j in range(GB)]
        for half in range(2):
            x = jnp.concatenate([t[K * half : K * half + K] for t in tiles], 0).T
            hi, lo = split(x)
            vt[half, :, pl.ds(pl.multiple_of(2 * wide * g, S), wide)] = hi
            vt[half, :, pl.ds(pl.multiple_of(2 * wide * g + wide, S), wide)] = lo
        return carry

    lax.fori_loop(0, NGB, basis_block, 0)

    field_o[...] = jnp.zeros_like(field_o)

    def field_group(g):
        parts = []
        for i in range(GS):
            s = GS * g + i
            rr = rrr[s]
            x = rbuf[s]
            parts.append(jnp.where(rows48f < rr[0:1], x[:K], 0.0))
            parts.append(jnp.where(rows48f < rr[1:2], flipped(x[MID:]), 0.0))
        hi, lo = split(jnp.concatenate(parts, 0))
        at = pl.ds(pl.multiple_of(GS * 2 * K * g, S), GS * 2 * K)
        p = dot(u2[0, :, at], jnp.concatenate([hi, lo], 1))
        q = dot(u2[1, :, at], hi)
        field_o[...] += p[:, :S] + p[:, S:] + q

    def field_loop(k, c):
        g = (mg - k + NG) % NG
        wait_for(rbuf, rsem.at[g], GS)
        field_group(g)
        return c

    lax.fori_loop(1, NG, field_loop, 0)
    own.wait()
    wait_for(rbuf, rsem.at[mg], GS - 1)
    field_group(mg)

    def at_well(w, c):
        gacc[pl.ds(w, 1), :] = field_o[pl.ds(wells_s[w], 1), :]
        return c

    lax.fori_loop(0, WPT, at_well, 0)
    obscopy.wait()
    e = jnp.exp(gacc[:WPT])
    wag[me] = (e - obs[...]) * e / 0.25
    gacc[...] = jnp.zeros_like(gacc)

    def gradient_group(g):
        pa, pb = [], []
        for j in range(GB):
            c = col(my + NY - j // 2, mz + NZ - steps_z(g), mc + j)
            q = slot_s[c]
            m = rbuf2[GB * g + j]
            hi = m.astype(BF16).astype(F32)
            lo = m - hi
            turned = pltpu.roll(lo, WPT, 1)
            one = jnp.where(left, hi[:TOP], turned[:TOP])
            end = jnp.where(left8, hi[TOP:], turned[TOP:])
            turned = pltpu.roll(hi, WPT, 1)
            two = jnp.where(left, turned[:TOP], lo[:TOP])
            end2 = jnp.where(left8, turned[TOP:], lo[TOP:])
            end = jnp.where(upper8, end, pltpu.roll(end2, 4, 0))
            rows = jnp.concatenate([one, two, end], 0).astype(BF16)
            whi, wlo = split(wag[c])
            w2 = jnp.concatenate(
                [
                    jnp.concatenate([whi, wlo], 1),
                    jnp.concatenate([whi, jnp.zeros_like(whi)], 1),
                ],
                0,
            )
            p = dot(rows, w2)
            adj = p[:, :S] + p[:, S:]
            pa.append(jnp.where(rows48 < ranks_s[0, q], adj[:K], 0.0))
            pb.append(jnp.where(rows48 < ranks_s[1, q], flipped(adj[MID:RPAIR]), 0.0))
        at = pl.ds(2 * GB * K * g, 2 * GB * K)
        for half, parts in ((0, pa), (1, pb)):
            hi, lo = split(jnp.concatenate(parts, 0))
            both = jnp.concatenate(
                [
                    jnp.concatenate([hi, lo], 1),
                    jnp.concatenate([hi, jnp.zeros_like(hi)], 1),
                ],
                0,
            )
            p = dot(vt[half, :, at], both)
            gacc[B * half : B * half + B, :] += p[:, :S] + p[:, S:]

    partner = col(my, mz, mc + 1)

    def pass_on(s, rs, to):
        copy_to(wag.at[s], wag.at[s], agsem, rs, to).start()

    def source(dy, i):
        return col(my + NY - dy, mz + NZ - steps_z(i), mc)

    def own_piece(i):
        for dy in (1, 3):
            pass_on(source(0, i), yrsem.at[dy * NZ + i], col(my + dy, mz, mc))
        pass_on(source(0, i), prsem.at[OTHER[i]], partner)

    def along(way):
        return col(my, mz + NZ + way, mc)

    for i in range(1, 5):
        pass_on(me, zrsem.at[i], along(steps_z(i)))
    own_piece(0)
    for step in range(NZ + LAG):
        i = step
        if 1 <= i < NZ:
            wait_for(wag, zrsem.at[i], 1)
            if i == 3:
                pass_on(source(0, i), zrsem.at[5], along(ahead))
                pass_on(source(0, i), zrsem.at[7], along(2 * ahead))
            if i == 4:
                pass_on(source(0, i), zrsem.at[6], along(-ahead))
            own_piece(i)
        i = step - 2
        if 0 <= i < NZ:
            for dy in (1, 3):
                wait_for(wag, yrsem.at[dy * NZ + i], 1)
                if dy == (3 if i % 2 else 1):
                    pass_on(source(dy, i), yrsem.at[2 * NZ + i], col(my + dy, mz, mc))
                pass_on(source(dy, i), prsem.at[OTHER[i]], partner)
        i = step - 4
        if 0 <= i < NZ:
            wait_for(wag, yrsem.at[2 * NZ + i], 1)
            pass_on(source(2, i), prsem.at[OTHER[i]], partner)
        send_wells(PACE)
        i = step - LAG
        if 0 <= i < NZ:
            wait_for(wag, prsem.at[i], NY)
            if i == 0:
                own2.wait()
            wait_wells(rsem2.at[i], GB if i else GB - 1)
            gradient_group(i)

    part = 2 * B // NR

    def exchange(d):
        to = (row + d) % NR
        return pltpu.make_async_remote_copy(
            src_ref=gacc.at[pl.ds(pl.multiple_of(part * to, part), part)],
            dst_ref=xrecv.at[d - 1],
            send_sem=xssem.at[d - 1],
            recv_sem=xrsem.at[d - 1],
            device_id=(me, to),
            device_id_type=MESH,
        )

    moves = [exchange(d) for d in range(1, NR)]
    for m in moves:
        m.start()
    mine = pl.ds(pl.multiple_of(part * row, part), part)
    total = lat[mine, :] + gacc[mine, :]
    for d in range(1, NR):
        moves[d - 1].wait_recv()
        total += xrecv[d - 1]
    grad_o[...] = total
    for m in moves:
        m.wait_send()
    wait_for(sbuf, ssem, NC - 1)
    wait_wells(ssem2, NC - 1)
    wait_for(rrs, rrssem, NC - 1)
    wait_for(wag, agsem, NC - 1)


def hand_over(field, gradient, field_o, grad_o):
    field_o[...] = field[...]
    grad_o[...] = gradient[...]


def on_device(latent, v_basis, u_basis, ranks, slot_row, wells, observed):
    vmem = pl.BlockSpec(memory_space=pltpu.VMEM)
    smem = pl.BlockSpec(memory_space=pltpu.SMEM)
    anywhere = pl.BlockSpec(memory_space=pl.ANY)
    dma = pltpu.SemaphoreType.DMA
    field, gradient = pl.pallas_call(
        kernel,
        name="tlr",
        out_shape=(
            pltpu.VMEM((B, S), F32),
            pltpu.VMEM((2 * B // NR, S), F32),
        ),
        in_specs=[smem, smem, smem, anywhere, anywhere, anywhere, anywhere],
        out_specs=(vmem, vmem),
        scratch_shapes=[
            pltpu.VMEM((NC, 2 * K, B), F32),
            pltpu.VMEM((B, NC * 2 * K), F32),
            pltpu.VMEM((2 * B, 2 * S), BF16),
            pltpu.VMEM((2, B, NC * 2 * K), BF16),
            pltpu.VMEM((2 * WPT, NC * 2 * K), F32),
            pltpu.VMEM((NC * 2 * K, S), F32),
            pltpu.VMEM((2, B, NC * 2 * K), BF16),
            pltpu.VMEM((NC, RPAIR, S), F32),
            pltpu.VMEM((NC, RPAIR, S), F32),
            pltpu.VMEM((NC, HALF, S), F32),
            pltpu.VMEM((NC, HALF, S), F32),
            pltpu.VMEM((NC, 2, S), F32),
            pltpu.VMEM((NC, 2, S), F32),
            pltpu.VMEM((NC, WPT, S), F32),
            pltpu.VMEM((2 * B, S), F32),
            pltpu.VMEM((NR - 1, 2 * B // NR, S), F32),
            pltpu.VMEM((2 * B, S), F32),
            pltpu.VMEM((WPT, S), F32),
            dma, dma, dma, dma, dma, dma, dma, dma((NG,)), dma, dma, dma, dma((NGB,)),
            dma, dma((NZ,)), dma((NY * NZ,)), dma((NZ,)), pltpu.SMEM((NC,), jnp.int32),
            dma((NR - 1,)), dma((NR - 1,)),
        ],
        compiler_params=pltpu.CompilerParams(
            collective_id=0, has_side_effects=True, vmem_limit_bytes=60 * 2**20
        ),
    )(
        slot_row[0],
        ranks[:, 0].T,
        wells[0, 0],
        latent,
        observed[0, 0],
        v_basis.reshape(NC, 2 * K, B),
        u_basis[0, 0],
    )
    field, gradient = pl.pallas_call(
        hand_over,
        name="hand_over",
        out_shape=(
            jax.ShapeDtypeStruct(field.shape, F32),
            jax.ShapeDtypeStruct(gradient.shape, F32),
        ),
        in_specs=[vmem, vmem],
        out_specs=(vmem, vmem),
    )(
        pltpu.with_memory_space_constraint(field, pltpu.VMEM),
        pltpu.with_memory_space_constraint(gradient, pltpu.VMEM),
    )
    return (field[None, None], gradient)


def solution(mesh):
    placed = (
        P("col", None),
        P(None, "row", "col", None, None),
        P("col", "row", None, None),
        P(None, "row", "col"),
        P("row", None),
        P("col", "row", None),
        P("col", "row", None, None),
    )
    return jax.shard_map(
        on_device,
        mesh=mesh,
        in_specs=placed,
        out_specs=(P("col", "row", None, None), P(("col", "row"), None)),
        check_vma=False,
    )
```

```python
import jax
import jax.numpy as jnp
from jax import lax
from jax.experimental import pallas as pl
from jax.experimental.pallas import tpu as pltpu
from jax.sharding import PartitionSpec as P

MESH = pl.DeviceIdType.MESH
F32, BF16 = jnp.float32, jnp.bfloat16
K = 48
RPAIR = 72
MID = RPAIR - K
S = 128
B = 256
NC = 64
NR = 4
GS = 4
NG = NC // GS
GB = 8
NGB = NC // GB
NY = 4
NZ = 8
WPT = 64
HALF = 40
TOP = 32
EARLY = 15
PACE = 10
LAG = 6
ORDER = [GB * g + n for g in (0, 7, 6, 1, 2, 3, 4, 5) for n in range(GB)]
OTHER = (0, 2, 1, 4, 3, 6, 5, 7)


def split(x):
    hi = x.astype(BF16)
    return hi, (x - hi.astype(F32)).astype(BF16)


def dot(a, b):
    return jnp.dot(a, b, preferred_element_type=F32)


def flipped(x):
    v = x.reshape(K // 8, 8, S)
    i = lax.broadcasted_iota(jnp.int32, (K // 8, 8, S), 1)
    for step in (1, 2, 4):
        v = jnp.where((i & step) == 0, pltpu.roll(v, 8 - step, 1), pltpu.roll(v, step, 1))
    return jnp.concatenate([v[K // 8 - 1 - t] for t in range(K // 8)], 0)


def pack(a, b):
    r = flipped(b)
    return jnp.concatenate([a[:MID], a[MID:] + r[:MID], r[MID:]], 0)


def kernel(
    slot_s, ranks_s, wells_s, lat_hbm, obs_hbm, v_hbm, u_hbm, field_o, grad_o,
    v, u, l2, u2, ur, ut, vt, sbuf, rbuf, sbuf2, rbuf2, rrs, rrr, wag, gacc, xrecv,
    lat, obs, latsem, obssem, vsem, usem, lsem, lsem2, ssem, rsem, rrssem, rrrsem, ssem2, rsem2, agsem, zrsem, yrsem, prsem, source_s, xssem, xrsem,
):
    me = lax.axis_index("col")
    row = lax.axis_index("row")
    mg = me // GS
    mu = me % GS
    my = me // (NZ * 2)
    mz = me // 2 % NZ
    mc = me % 2
    latcopy = pltpu.make_async_copy(lat_hbm, lat, latsem)
    latcopy.start()
    vcopy = pltpu.make_async_copy(v_hbm, v, vsem)
    vcopy.start()
    ucopy = pltpu.make_async_copy(u_hbm, u, usem)

    barrier = pltpu.get_barrier_semaphore()

    def greet(i, c):
        pl.semaphore_signal(barrier, inc=1, device_id=((me + i) % NC, row), device_id_type=MESH)
        return c

    lax.fori_loop(1, NC, greet, 0)
    for i in range(1, NR):
        pl.semaphore_signal(barrier, inc=1, device_id=(me, (row + i) % NR), device_id_type=MESH)

    rows48 = lax.broadcasted_iota(jnp.int32, (K, S), 0)
    rows48f = rows48.astype(F32)

    latcopy.wait()
    lhi, llo = split(lat[...])
    l2[:, :S] = lhi
    l2[:, S:] = llo

    def peer(k, i):
        return GS * ((mg + k) % NG) + (i + mu) % GS

    def copy_to(src, dst, ss, rs, col):
        return pltpu.make_async_remote_copy(
            src_ref=src,
            dst_ref=dst,
            send_sem=ss,
            recv_sem=rs,
            device_id=(col, row),
            device_id_type=MESH,
        )

    def wait_for(buf, sem, n):
        pltpu.make_async_copy(buf.at[pl.ds(0, n)], buf.at[pl.ds(0, n)], sem).wait()

    def rank_row(k, c):
        for i in range(GS):
            q = slot_s[peer(k, i)]
            first = lax.broadcasted_iota(jnp.int32, (2, S), 0) == 0
            rrs[GS * k + i] = jnp.where(first, ranks_s[0, q], ranks_s[1, q]).astype(F32)
        return c

    lax.fori_loop(0, NG, rank_row, 0)
    rrr[me] = rrs[0]

    def col(y, z, c):
        return y % NY * (NZ * 2) + z % NZ * 2 + c % 2

    ahead = 1 - 2 * mc

    def steps_z(i):
        return (ahead if i % 2 else -ahead) * ((i + 1) // 2)

    for i in range(NGB):
        for n in range(GB):
            source_s[GB * i + n] = col(my + NY - n // 2, mz + NZ - steps_z(i), mc + n)

    vcopy.wait()
    ucopy.start()
    obscopy = pltpu.make_async_copy(obs_hbm, obs, obssem)
    obscopy.start()

    def products(x, half):
        hi, lo = split(x)
        n = x.shape[0]
        p = dot(jnp.concatenate([hi, lo], 0), l2[B * half : B * half + B, :])
        return p[:n, :S] + p[:n, S:] + p[n:, :S]

    def forward(k):
        qs = [slot_s[peer(k, i)] for i in range(GS)]
        tiles = [v[q] for q in qs]
        a = products(jnp.concatenate([x[:K] for x in tiles], 0), 0)
        b = products(jnp.concatenate([x[K:] for x in tiles], 0), 1)
        for i in range(GS):
            ai = jnp.where(rows48 < ranks_s[0, qs[i]], a[K * i : K * i + K], 0.0)
            bi = jnp.where(rows48 < ranks_s[1, qs[i]], b[K * i : K * i + K], 0.0)
            sbuf[GS * k + i] = pack(ai, bi)

    def send(k, i):
        copy_to(sbuf.at[GS * k + i], rbuf.at[me], ssem, rsem.at[mg], peer(k, i)).start()

    def send_ranks(k, i):
        copy_to(rrs.at[GS * k + i], rrr.at[me], rrssem, rrrsem, peer(k, i)).start()

    forward(0)
    pl.semaphore_wait(barrier, NC - 1 + NR - 1)
    for i in range(1, GS):
        send_ranks(0, i)

    def ranks_loop(k, c):
        for i in range(GS):
            send_ranks(k, i)
        return c

    lax.fori_loop(1, NG, ranks_loop, 0)

    forward(1)
    own = pltpu.make_async_copy(sbuf.at[0], rbuf.at[me], lsem)
    own.start()
    for i in range(1, GS):
        send(0, i)

    def forward_loop(k, c):
        forward(k)
        for i in range(GS):
            send(k - 1, i)
        return c

    lax.fori_loop(2, NG, forward_loop, 0)
    for i in range(GS):
        send(NG - 1, i)

    ucopy.wait()

    def well_row(w, c):
        at = u[pl.ds(wells_s[w], 1), :]
        ur[pl.ds(w, 1), :] = at
        ur[pl.ds(w + WPT, 1), :] = at
        return c

    lax.fori_loop(0, WPT, well_row, 0)

    def well_block(c, carry):
        at = pl.ds(pl.multiple_of(S * c, S), S)
        ut[at, :] = ur[:, at].T
        return carry

    lax.fori_loop(0, NC * 2 * K // S, well_block, 0)
    wait_for(rrr, rrrsem, NC - 1)
    left = lax.broadcasted_iota(jnp.int32, (TOP, S), 1) < WPT
    left8 = lax.broadcasted_iota(jnp.int32, (8, S), 1) < WPT
    upper8 = lax.broadcasted_iota(jnp.int32, (8, S), 0) < 4

    def pack_wells(j, carry):
        rr = rrr[j]
        x = ut[pl.ds(pl.multiple_of(2 * K * j, 2 * K), 2 * K), :]
        p = pack(
            jnp.where(rows48f < rr[0:1], x[:K], 0.0),
            jnp.where(rows48f < rr[1:2], x[K:], 0.0),
        )
        sbuf2[j, :TOP] = jnp.where(left, p[:TOP], p[TOP : 2 * TOP])
        end = p[2 * TOP :]
        sbuf2[j, TOP:] = jnp.where(left8, end, pltpu.roll(end, 4, 0))
        return carry

    lax.fori_loop(0, NC, pack_wells, 0)

    def part2(buf, s):
        return buf.at[s, pl.ds(0, RPAIR // 2)]

    def wait_wells(sem, n):
        both = rbuf2.at[pl.ds(0, n), pl.ds(0, RPAIR // 2)]
        pltpu.make_async_copy(both, both, sem).wait()

    own2 = pltpu.make_async_copy(part2(sbuf2, me), part2(rbuf2, 0), lsem2)
    own2.start()
    waiting = [n for n in ORDER if n]

    def send_wells(count):
        for n in waiting[:count]:
            dz = steps_z(n // GB) * (1 - 2 * (n % 2))
            to = col(my + n % GB // 2, mz + NZ + dz, mc + n)
            copy_to(part2(sbuf2, to), part2(rbuf2, n), ssem2, rsem2.at[n // GB], to).start()
        del waiting[:count]

    send_wells(EARLY)

    def split_u(c, carry):
        at = pl.ds(pl.multiple_of(512 * c, 512), 512)
        hi, lo = split(u[:, at])
        u2[0, :, at] = hi
        u2[1, :, at] = lo
        return carry

    lax.fori_loop(0, NC * 2 * K // 512, split_u, 0)

    def basis_block(g, carry):
        wide = GB * K
        tiles = [v[slot_s[source_s[GB * g + j]]] for j in range(GB)]
        for half in range(2):
            x = jnp.concatenate([t[K * half : K * half + K] for t in tiles], 0).T
            hi, lo = split(x)
            vt[half, :, pl.ds(pl.multiple_of(2 * wide * g, S), wide)] = hi
            vt[half, :, pl.ds(pl.multiple_of(2 * wide * g + wide, S), wide)] = lo
        return carry

    lax.fori_loop(0, NGB, basis_block, 0)

    field_o[...] = jnp.zeros_like(field_o)

    def field_group(g):
        parts = []
        for i in range(GS):
            s = GS * g + i
            rr = rrr[s]
            x = rbuf[s]
            parts.append(jnp.where(rows48f < rr[0:1], x[:K], 0.0))
            parts.append(jnp.where(rows48f < rr[1:2], flipped(x[MID:]), 0.0))
        hi, lo = split(jnp.concatenate(parts, 0))
        at = pl.ds(pl.multiple_of(GS * 2 * K * g, S), GS * 2 * K)
        p = dot(u2[0, :, at], jnp.concatenate([hi, lo], 1))
        q = dot(u2[1, :, at], hi)
        field_o[...] += p[:, :S] + p[:, S:] + q

    def field_loop(k, c):
        g = (mg - k + NG) % NG
        wait_for(rbuf, rsem.at[g], GS)
        field_group(g)
        return c

    lax.fori_loop(1, NG, field_loop, 0)
    own.wait()
    wait_for(rbuf, rsem.at[mg], GS - 1)
    field_group(mg)

    def at_well(w, c):
        gacc[pl.ds(w, 1), :] = field_o[pl.ds(wells_s[w], 1), :]
        return c

    lax.fori_loop(0, WPT, at_well, 0)
    obscopy.wait()
    e = jnp.exp(gacc[:WPT])
    wag[me] = (e - obs[...]) * e / 0.25
    gacc[...] = jnp.zeros_like(gacc)

    def gradient_group(g):
        pa, pb = [], []
        for j in range(GB):
            c = col(my + NY - j // 2, mz + NZ - steps_z(g), mc + j)
            q = slot_s[c]
            m = rbuf2[GB * g + j]
            hi = m.astype(BF16).astype(F32)
            lo = m - hi
            turned = pltpu.roll(lo, WPT, 1)
            one = jnp.where(left, hi[:TOP], turned[:TOP])
            end = jnp.where(left8, hi[TOP:], turned[TOP:])
            turned = pltpu.roll(hi, WPT, 1)
            two = jnp.where(left, turned[:TOP], lo[:TOP])
            end2 = jnp.where(left8, turned[TOP:], lo[TOP:])
            end = jnp.where(upper8, end, pltpu.roll(end2, 4, 0))
            rows = jnp.concatenate([one, two, end], 0).astype(BF16)
            whi, wlo = split(wag[c])
            w2 = jnp.concatenate(
                [
                    jnp.concatenate([whi, wlo], 1),
                    jnp.concatenate([whi, jnp.zeros_like(whi)], 1),
                ],
                0,
            )
            p = dot(rows, w2)
            adj = p[:, :S] + p[:, S:]
            pa.append(jnp.where(rows48 < ranks_s[0, q], adj[:K], 0.0))
            pb.append(jnp.where(rows48 < ranks_s[1, q], flipped(adj[MID:RPAIR]), 0.0))
        at = pl.ds(2 * GB * K * g, 2 * GB * K)
        for half, parts in ((0, pa), (1, pb)):
            hi, lo = split(jnp.concatenate(parts, 0))
            both = jnp.concatenate(
                [
                    jnp.concatenate([hi, lo], 1),
                    jnp.concatenate([hi, jnp.zeros_like(hi)], 1),
                ],
                0,
            )
            p = dot(vt[half, :, at], both)
            gacc[B * half : B * half + B, :] += p[:, :S] + p[:, S:]

    partner = col(my, mz, mc + 1)

    def pass_on(s, rs, to):
        copy_to(wag.at[s], wag.at[s], agsem, rs, to).start()

    def source(dy, i):
        return col(my + NY - dy, mz + NZ - steps_z(i), mc)

    def own_piece(i):
        for dy in (1, 3):
            pass_on(source(0, i), yrsem.at[dy * NZ + i], col(my + dy, mz, mc))
        pass_on(source(0, i), prsem.at[OTHER[i]], partner)

    def along(way):
        return col(my, mz + NZ + way, mc)

    for i in range(1, 5):
        pass_on(me, zrsem.at[i], along(steps_z(i)))
    own_piece(0)
    for step in range(NZ + LAG):
        i = step
        if 1 <= i < NZ:
            wait_for(wag, zrsem.at[i], 1)
            if i == 3:
                pass_on(source(0, i), zrsem.at[5], along(ahead))
                pass_on(source(0, i), zrsem.at[7], along(2 * ahead))
            if i == 4:
                pass_on(source(0, i), zrsem.at[6], along(-ahead))
            own_piece(i)
        i = step - 2
        if 0 <= i < NZ:
            for dy in (1, 3):
                wait_for(wag, yrsem.at[dy * NZ + i], 1)
                if dy == (3 if i % 2 else 1):
                    pass_on(source(dy, i), yrsem.at[2 * NZ + i], col(my + dy, mz, mc))
                pass_on(source(dy, i), prsem.at[OTHER[i]], partner)
        i = step - 4
        if 0 <= i < NZ:
            wait_for(wag, yrsem.at[2 * NZ + i], 1)
            pass_on(source(2, i), prsem.at[OTHER[i]], partner)
        send_wells(PACE)
        i = step - LAG
        if 0 <= i < NZ:
            wait_for(wag, prsem.at[i], NY)
            if i == 0:
                own2.wait()
            wait_wells(rsem2.at[i], GB if i else GB - 1)
            gradient_group(i)

    part = 2 * B // NR

    def exchange(d):
        to = (row + d) % NR
        return pltpu.make_async_remote_copy(
            src_ref=gacc.at[pl.ds(pl.multiple_of(part * to, part), part)],
            dst_ref=xrecv.at[d - 1],
            send_sem=xssem.at[d - 1],
            recv_sem=xrsem.at[d - 1],
            device_id=(me, to),
            device_id_type=MESH,
        )

    moves = [exchange(d) for d in range(1, NR)]
    for m in moves:
        m.start()
    mine = pl.ds(pl.multiple_of(part * row, part), part)
    total = lat[mine, :] + gacc[mine, :]
    for d in range(1, NR):
        moves[d - 1].wait_recv()
        total += xrecv[d - 1]
    grad_o[...] = total
    for m in moves:
        m.wait_send()
    wait_for(sbuf, ssem, NC - 1)
    wait_wells(ssem2, NC - 1)
    wait_for(rrs, rrssem, NC - 1)
    wait_for(wag, agsem, NC - 1)


def hand_over(field, gradient, field_o, grad_o):
    field_o[...] = field[...]
    grad_o[...] = gradient[...]


def on_device(latent, v_basis, u_basis, ranks, slot_row, wells, observed):
    vmem = pl.BlockSpec(memory_space=pltpu.VMEM)
    smem = pl.BlockSpec(memory_space=pltpu.SMEM)
    anywhere = pl.BlockSpec(memory_space=pl.ANY)
    dma = pltpu.SemaphoreType.DMA
    field, gradient = pl.pallas_call(
        kernel,
        name="tlr",
        out_shape=(
            pltpu.VMEM((B, S), F32),
            pltpu.VMEM((2 * B // NR, S), F32),
        ),
        in_specs=[smem, smem, smem, anywhere, anywhere, anywhere, anywhere],
        out_specs=(vmem, vmem),
        scratch_shapes=[
            pltpu.VMEM((NC, 2 * K, B), F32),
            pltpu.VMEM((B, NC * 2 * K), F32),
            pltpu.VMEM((2 * B, 2 * S), BF16),
            pltpu.VMEM((2, B, NC * 2 * K), BF16),
            pltpu.VMEM((2 * WPT, NC * 2 * K), F32),
            pltpu.VMEM((NC * 2 * K, S), F32),
            pltpu.VMEM((2, B, NC * 2 * K), BF16),
            pltpu.VMEM((NC, RPAIR, S), F32),
            pltpu.VMEM((NC, RPAIR, S), F32),
            pltpu.VMEM((NC, HALF, S), F32),
            pltpu.VMEM((NC, HALF, S), F32),
            pltpu.VMEM((NC, 2, S), F32),
            pltpu.VMEM((NC, 2, S), F32),
            pltpu.VMEM((NC, WPT, S), F32),
            pltpu.VMEM((2 * B, S), F32),
            pltpu.VMEM((NR - 1, 2 * B // NR, S), F32),
            pltpu.VMEM((2 * B, S), F32),
            pltpu.VMEM((WPT, S), F32),
            dma, dma, dma, dma, dma, dma, dma, dma((NG,)), dma, dma, dma, dma((NGB,)),
            dma, dma((NZ,)), dma((NY * NZ,)), dma((NZ,)), pltpu.SMEM((NC,), jnp.int32),
            dma((NR - 1,)), dma((NR - 1,)),
        ],
        compiler_params=pltpu.CompilerParams(
            collective_id=0, has_side_effects=True, vmem_limit_bytes=60 * 2**20
        ),
    )(
        slot_row[0],
        ranks[:, 0].T,
        wells[0, 0],
        latent,
        observed[0, 0],
        v_basis.reshape(NC, 2 * K, B),
        u_basis[0, 0],
    )
    field, gradient = pl.pallas_call(
        hand_over,
        name="hand_over",
        out_shape=(
            jax.ShapeDtypeStruct(field.shape, F32),
            jax.ShapeDtypeStruct(gradient.shape, F32),
        ),
        in_specs=[vmem, vmem],
        out_specs=(vmem, vmem),
    )(
        pltpu.with_memory_space_constraint(field, pltpu.VMEM),
        pltpu.with_memory_space_constraint(gradient, pltpu.VMEM),
    )
    return (field[None, None], gradient)


def solution(mesh):
    placed = (
        P("col", None),
        P(None, "row", "col", None, None),
        P("col", "row", None, None),
        P(None, "row", "col"),
        P("row", None),
        P("col", "row", None),
        P("col", "row", None, None),
    )
    return jax.shard_map(
        on_device,
        mesh=mesh,
        in_specs=placed,
        out_specs=(P("col", "row", None, None), P(("col", "row"), None)),
        check_vma=False,
    )
```
